256 devices in a mesh: sample: 4 (over z_lo, core), space: 64 (over y, z_hi, x).
Axes of the slice: x: 4, y: 4, z: 8 (z_hi: 4, z_lo: 2; z = z_hi * 2 + z_lo), core: 2. Of those that a mesh axis runs over, the one named last changes fastest.
Arguments:
- acts: bfloat16 [8, 64, 16, 8, 8, 128], P('sample', 'space'), may hold values from -6 to 6
- weight: float32 [3456, 128], P('space'), may hold values from -0.109375 to 0.109375
- moment: float32 [3456, 128], P('space'), may hold values from -3 to 3
- second: float32 [3456, 128], P('space'), may hold values from 0.05 to 2
- cotangent: bfloat16 [8, 64, 16, 8, 8, 128], P('sample', 'space'), may hold values from -6 to 6
Outputs:
- output: bfloat16 [8, 64, 16, 8, 8, 128], P('sample', 'space')
- input_grad: bfloat16 [8, 64, 16, 8, 8, 128], P('sample', 'space')
- weight_grad: float32 [3456, 128], P('space')
- new_weight: float32 [3456, 128], P('space')
- new_moment: float32 [3456, 128], P('space')
- new_second: float32 [3456, 128], P('space')
The draws below stay inside these ranges and needn't reach their ends.
All inputs are finite; a program needn't handle non-finite values.
Results may differ from the reference program's by a relative error of at most 0.0062.
Values may be sent and summed in bfloat16 or wider, within the bound.
No kernel may reach another device: no remote copies, remote signals or barrier semaphores. Data moves between devices by JAX's collectives and lax.ppermute only.
A program may use at most 64 MiB of HBM per device.

```python
import math
import jax
import jax.numpy as jnp
from jax import lax

CH = 128
BX = 16
BY = 8
BZ = 8
GY = 2
GZ = 4
BRICKS = 64
BATCH = 8


def block_scale(rng, extent, pieces, low, high):
    factor_of = 1.0
    for position, shards_of in pieces:
        draws = jax.random.uniform(jax.random.fold_in(jax.random.fold_in(rng, 6), position), (shards_of,), jnp.float32, low / len(pieces), high / len(pieces))
        factor_of = factor_of * jnp.repeat(jnp.exp(draws), extent[position] // shards_of).reshape((-1,) + (1,) * (len(extent) - 1 - position))
    return factor_of


def noise(own_key, dims, width, most, cuts=(), dtype=jnp.bfloat16):
    array = jax.random.normal(own_key, dims, jnp.float32) * width
    if len(cuts) > 0:
        array = block_scale(own_key, dims, cuts, -0.22, 0.18) * array
    return jnp.clip(array, min=-most, max=most).astype(dtype)


def setup_inputs(seed: int = 0) -> dict:
    key_of = jax.random.split(jax.random.key(seed), 6)
    acts = noise(key_of[0], (BATCH, BRICKS, BX, BY, BZ, CH), 1.0, 6.0, ((0, 4), (1, 64)))
    weight = noise(key_of[1], (27 * CH, CH), (27 * CH) ** -0.5, 0.109375, ((0, 64),), jnp.float32)
    moment = noise(key_of[2], (27 * CH, CH), 0.5, 3.0, ((0, 64),), jnp.float32)
    second = jnp.clip(jnp.exp(math.log(2.0) - 3.6888794 * jax.random.uniform(key_of[3], (27 * CH, CH), jnp.float32) ** block_scale(key_of[3], (27 * CH, CH), ((0, 64),), -0.2, 0.2)), 0.05, 2.0)
    cotangent = noise(key_of[4], (BATCH, BRICKS, BX, BY, BZ, CH), 1.0, 6.0, ((0, 4), (1, 64)))
    return {"acts": acts, "weight": weight, "moment": moment, "second": second, "cotangent": cotangent}


root_coef = 0.7978845608
cubic_coef = 0.044715

def to_crop(field):
    nb, nr, sx, sy, sz, nc = field.shape
    groups = nr // (GY * GZ)
    shaped = field.reshape(nb, groups, GY, GZ, sx, sy, sz, nc)
    shaped = shaped.transpose(0, 1, 4, 2, 5, 3, 6, 7)
    return shaped.reshape(nb, groups * sx, GY * sy, GZ * sz, nc)

def to_bricks(field):
    nb, nx, ny, nz, nc = field.shape
    groups = nx // BX
    shaped = field.reshape(nb, groups, BX, GY, BY, GZ, BZ, nc)
    shaped = shaped.transpose(0, 1, 3, 5, 2, 4, 6, 7)
    return shaped.reshape(nb, groups * GY * GZ, BX, BY, BZ, nc)

def convolve(field, kernel, padding):
    return lax.conv_general_dilated(field, kernel, (1, 1, 1), padding, dimension_numbers=('NDHWC', 'DHWIO', 'NDHWC'), preferred_element_type=jnp.float32)

def activate(pre):
    inner = root_coef * (pre + cubic_coef * pre * pre * pre)
    tval = jnp.tanh(inner)
    value = 0.5 * pre * (1.0 + tval)
    slope = 0.5 * (1.0 + tval) + 0.5 * pre * (1.0 - tval * tval) * root_coef * (1.0 + 3.0 * cubic_coef * pre * pre)
    return (value, slope)

def kernel_terms(padded, grad_pre):
    nx, ny, nz = (grad_pre.shape[1], grad_pre.shape[2], grad_pre.shape[3])
    terms = []
    for kx in range(3):
        for ky in range(3):
            for kz in range(3):
                window = padded[:, kx:kx + nx, ky:ky + ny, kz:kz + nz, :]
                terms.append(lax.dot_general(window, grad_pre, (((0, 1, 2, 3), (0, 1, 2, 3)), ((), ())), preferred_element_type=jnp.float32))
    stacked = jnp.stack(terms, 0)
    return stacked.reshape(27 * stacked.shape[1], stacked.shape[2])

def adam(weight, moment, second, grad):
    new_moment = 0.9 * moment + 0.1 * grad
    new_second = 0.999 * second + 0.001 * grad * grad
    first_fix = 1.0 - 0.9 ** 10
    second_fix = 1.0 - 0.999 ** 10
    new_weight = weight - 0.001 * (new_moment / first_fix) / (jnp.sqrt(new_second / second_fix) + 1e-08)
    return (new_weight, new_moment, new_second)

def reference(acts, weight, moment, second, cotangent):
    crop = to_crop(acts)
    grad_out = to_crop(cotangent)
    channels = weight.shape[1]
    kernel = weight.astype(jnp.bfloat16).reshape(3, 3, 3, channels, channels)
    pad = [(1, 1), (1, 1), (1, 1)]
    pre = convolve(crop, kernel, pad)
    value, slope = activate(pre)
    output = value.astype(jnp.bfloat16)
    grad_pre = (grad_out.astype(jnp.float32) * slope).astype(jnp.bfloat16)
    flipped = jnp.flip(kernel, (0, 1, 2)).transpose(0, 1, 2, 4, 3)
    input_grad = convolve(grad_pre, flipped, pad).astype(jnp.bfloat16)
    padded = jnp.pad(crop, ((0, 0), (1, 1), (1, 1), (1, 1), (0, 0)))
    total = crop.shape[0] * crop.shape[1] * crop.shape[2] * crop.shape[3]
    weight_grad = kernel_terms(padded, grad_pre) * float(total) ** (-0.5)
    new_weight, new_moment, new_second = adam(weight, moment, second, weight_grad)
    return (to_bricks(output), to_bricks(input_grad), weight_grad, new_weight, new_moment, new_second)
```

```python
import jax
import jax.numpy as jnp
from jax import lax
from jax.sharding import PartitionSpec as P

GY = 2
GZ = 4


root_coef = 0.7978845608
cubic_coef = 0.044715


def flip_pairs(count, bit):
    return [(i, i ^ bit) for i in range(count)]


def odd_pairs(count, stride, length):
    pairs = []
    for i in range(count):
        coord = i // stride % length
        other = coord + 1 if coord % 2 == 1 else coord - 1
        if 0 <= other < length:
            pairs.append((i, i + (other - coord) * stride))
    return pairs


def swap_layers(first, last, coord, stride, length):
    devices = lax.axis_size("space")
    even = coord % 2 == 0
    inner = lax.ppermute(jnp.where(even, last, first), "space", flip_pairs(devices, stride))
    if length == 2:
        outer = jnp.zeros_like(inner)
    else:
        outer = lax.ppermute(
            jnp.where(even, first, last), "space", odd_pairs(devices, stride, length)
        )
    return jnp.where(even, outer, inner), jnp.where(even, inner, outer)


def extend(field):
    place = lax.axis_index("space")
    groups = lax.axis_size("space") // (GY * GZ)
    coord_z = place % GZ
    coord_y = place // GZ % GY
    coord_x = place // (GZ * GY)
    for dim, stride, coord, count in (
        (3, 1, coord_z, GZ),
        (2, GZ, coord_y, GY),
        (1, GY * GZ, coord_x, groups),
    ):
        length = field.shape[dim]
        first_layer = lax.slice_in_dim(field, 0, 1, 1, dim)
        last_layer = lax.slice_in_dim(field, length - 1, length, 1, dim)
        below, above = swap_layers(first_layer, last_layer, coord, stride, count)
        field = jnp.concatenate([below, field, above], dim)
    return field


def convolve(field, kernel):
    return lax.conv_general_dilated(
        field,
        kernel,
        (1, 1, 1),
        "VALID",
        dimension_numbers=("NDHWC", "DHWIO", "NDHWC"),
        preferred_element_type=jnp.float32,
    )


def activate(pre):
    inner = root_coef * (pre + cubic_coef * pre * pre * pre)
    tval = jnp.tanh(inner)
    value = 0.5 * pre * (1.0 + tval)
    slope = 0.5 * (1.0 + tval) + 0.5 * pre * (1.0 - tval * tval) * root_coef * (
        1.0 + 3.0 * cubic_coef * pre * pre
    )
    return (value, slope)


def kernel_terms(padded, grad_pre):
    nx, ny, nz = (grad_pre.shape[1], grad_pre.shape[2], grad_pre.shape[3])
    terms = []
    for kx in range(3):
        for ky in range(3):
            for kz in range(3):
                window = padded[:, kx : kx + nx, ky : ky + ny, kz : kz + nz, :]
                terms.append(
                    lax.dot_general(
                        window,
                        grad_pre,
                        (((0, 1, 2, 3), (0, 1, 2, 3)), ((), ())),
                        preferred_element_type=jnp.float32,
                    )
                )
    stacked = jnp.stack(terms, 0)
    return stacked.reshape(27 * stacked.shape[1], stacked.shape[2])


def core_swap(value):
    return lax.ppermute(value, "sample", flip_pairs(lax.axis_size("sample"), 1))


def chip_swap(value):
    return lax.ppermute(value, "sample", flip_pairs(lax.axis_size("sample"), 2))


def halves_joined(mine, other, core, dim):
    low = jnp.where(core == 0, mine, other)
    high = jnp.where(core == 0, other, mine)
    return jnp.concatenate([low, high], dim)


def whole_kernel(rows, core):
    devices = lax.axis_size("space")
    half = rows.shape[0] // 2
    mine = lax.dynamic_slice_in_dim(rows, core * half, half, 0)
    copies = jnp.broadcast_to(mine, (devices, *mine.shape))
    got = lax.all_to_all(copies, "space", split_axis=0, concat_axis=0, tiled=True)
    other = core_swap(got)
    return halves_joined(got, other, core, 1)


def own_rows_sum(terms, core):
    devices = lax.axis_size("space")
    parts = terms.reshape(devices, -1, terms.shape[1])
    half = parts.shape[1] // 2
    mine = lax.dynamic_slice_in_dim(parts, core * half, half, 1)
    away = lax.dynamic_slice_in_dim(parts, (1 - core) * half, half, 1)
    chip = mine + core_swap(away.astype(jnp.bfloat16)).astype(jnp.float32)
    arrived = lax.all_to_all(
        chip.astype(jnp.bfloat16), "space", split_axis=0, concat_axis=0, tiled=True
    )
    owned = arrived.astype(jnp.float32).sum(axis=0)
    owned = owned + chip_swap(owned)
    return halves_joined(owned, core_swap(owned), core, 0)


def local(acts, weight, moment, second, cotangent):
    field = acts[:, 0]
    grad_out = cotangent[:, 0]
    channels = weight.shape[1]
    core = lax.axis_index("sample") % 2
    rows_bf = weight.astype(jnp.bfloat16)
    kernel = whole_kernel(rows_bf, core).reshape(3, 3, 3, channels, channels)
    padded = extend(field)
    pre = convolve(padded, kernel)
    value, slope = activate(pre)
    output = value.astype(jnp.bfloat16)
    grad_pre = (grad_out.astype(jnp.float32) * slope).astype(jnp.bfloat16)
    flipped = jnp.flip(kernel, (0, 1, 2)).transpose(0, 1, 2, 4, 3)
    grad_padded = extend(grad_pre)
    input_grad = convolve(grad_padded, flipped).astype(jnp.bfloat16)
    total = (
        field.shape[0]
        * lax.axis_size("sample")
        * lax.axis_size("space")
        * field.shape[1]
        * field.shape[2]
        * field.shape[3]
    )
    local_terms = kernel_terms(padded, grad_pre) * float(total) ** (-0.5)
    weight_grad = own_rows_sum(local_terms, core)
    new_moment = 0.9 * moment + 0.1 * weight_grad
    new_second = 0.999 * second + 0.001 * weight_grad * weight_grad
    first_fix = 1.0 - 0.9**10
    second_fix = 1.0 - 0.999**10
    new_weight = weight - 0.001 * (new_moment / first_fix) / (
        jnp.sqrt(new_second / second_fix) + 1e-08
    )
    return (output[:, None], input_grad[:, None], weight_grad, new_weight, new_moment, new_second)


def solution(mesh):
    in_specs = (
        P("sample", "space", None, None, None, None),
        P("space", None),
        P("space", None),
        P("space", None),
        P("sample", "space", None, None, None, None),
    )
    out_specs = (
        P("sample", "space", None, None, None, None),
        P("sample", "space", None, None, None, None),
        P("space", None),
        P("space", None),
        P("space", None),
        P("space", None),
    )
    return jax.shard_map(local, mesh=mesh, in_specs=in_specs, out_specs=out_specs, check_vma=False)
```

```python
import functools

import jax
import jax.numpy as jnp
from jax import lax
from jax.experimental import pallas as pl
from jax.experimental.pallas import tpu as pltpu
from jax.sharding import PartitionSpec as P

GY = 2
GZ = 4

root_coef = 0.7978845608
cubic_coef = 0.044715
bf16, f32 = jnp.bfloat16, jnp.float32


def activate(pre):
    square = pre * pre
    inner = root_coef * (pre + cubic_coef * pre * square)
    tval = jnp.tanh(inner)
    value = 0.5 * pre * (1.0 + tval)
    slope = 0.5 * (1.0 + tval) + 0.5 * pre * (1.0 - tval * tval) * root_coef * (
        1.0 + 3.0 * cubic_coef * square
    )
    return (value, slope)


def fill_windows(center, ylo, yhi, zlo, zhi, windows, layers):
    place = lax.broadcasted_iota(jnp.int32, (8, 128), 0)

    def one(x, _):
        rows = [ylo[0, x].astype(f32)] + [center[0, x, y].astype(f32) for y in range(8)] + [yhi[0, x].astype(f32)]
        low, high = zlo[0, x].astype(f32), zhi[0, x].astype(f32)
        shifted = [[], [], []]
        for yy in range(10):
            row = rows[yy]
            lo = jnp.broadcast_to(low[yy : yy + 1], (8, 128))
            hi = jnp.broadcast_to(high[yy : yy + 1], (8, 128))
            shifted[0].append(jnp.where(place == 0, lo, pltpu.roll(row, 1, 0)))
            shifted[1].append(row)
            shifted[2].append(jnp.where(place == 7, hi, pltpu.roll(row, 7, 0)))
        for ky in range(3):
            for kz in range(3):
                col = (ky * 3 + kz) * 128
                tile = jnp.concatenate(shifted[kz][ky : ky + 8], axis=0).astype(bf16)
                windows[x, :, col : col + 128] = tile
        return 0

    lax.fori_loop(0, layers, one, 0)


def forward_kernel(scale, core_ref, center, ylo, yhi, zlo, zhi, dy, mine, other,
                   out, dz, parts, kern_out, windows, rows, kern, dzs, total, values):
    step = pl.program_id(0)
    core = core_ref[0]

    @pl.when(step == 0)
    def _():
        def piece(s, _):
            a, b = mine[s].astype(f32), other[s].astype(f32)
            rows[pl.ds(54 * s, 27), :] = jnp.where(core == 0, a, b)
            rows[pl.ds(54 * s + 27, 27), :] = jnp.where(core == 0, b, a)
            return 0
        lax.fori_loop(0, 64, piece, 0)
        for kx in range(3):
            kern[kx] = rows[1152 * kx : 1152 * (kx + 1), :].astype(bf16)
            kern_out[kx] = kern[kx]

    fill_windows(center, ylo, yhi, zlo, zhi, windows, 20)

    def layer(i, _):
        x = 3 * i
        pre = jnp.zeros((192, 128), f32)
        for kx in range(3):
            lhs = windows[pl.ds(x + kx, 3)].reshape(192, 1152)
            pre += jnp.dot(lhs, kern[kx], preferred_element_type=f32)
        value, slope = activate(pre)
        grad = (dy[0, pl.ds(x, 3)].reshape(192, 128).astype(f32) * slope).astype(bf16)
        dz[0, pl.ds(x, 3)] = grad.reshape(3, 64, 128)
        values[pl.ds(x, 3)] = value.astype(bf16).reshape(3, 64, 128)
        return 0

    lax.fori_loop(0, 6, layer, 0)
    out[0] = values[1:17]
    own = dz[0, 1:17].reshape(1024, 128)
    dzs[...] = jnp.zeros_like(dzs)
    for kx in range(3):
        dzs[64 * kx : 64 * kx + 1024, 128 * kx : 128 * (kx + 1)] = own
    both = windows[1:19].reshape(1152, 1152)
    term = lax.dot_general(dzs[...], both, (((0,), (0,)), ((), ())), preferred_element_type=f32)

    @pl.when(step == 0)
    def _():
        total[...] = term

    @pl.when(step == 1)
    def _():
        whole = (total[...] + term) * scale
        for kx in range(3):
            for t in range(9):
                block = whole[128 * kx : 128 * (kx + 1), 128 * t : 128 * (t + 1)]
                row = (kx * 9 + t) * 128
                rows[row : row + 128, :] = block.T
        def piece(s, _):
            parts[0, s] = rows[pl.ds(54 * s, 27), :].astype(bf16)
            parts[1, s] = rows[pl.ds(54 * s + 27, 27), :].astype(bf16)
            return 0
        lax.fori_loop(0, 64, piece, 0)


def forward(core, center, ylo, yhi, zlo, zhi, dy, mine, other, scale):
    def crop(shape):
        return pl.BlockSpec((1, *shape[1:]), lambda b: (b,) + (0,) * (len(shape) - 1))
    def whole(shape):
        return pl.BlockSpec(shape, lambda b: (0,) * len(shape), pipeline_mode=pl.Buffered(1))
    ins = (center, ylo, yhi, zlo, zhi, dy)
    outs = [jax.ShapeDtypeStruct((2, 16, 64, 128), bf16), jax.ShapeDtypeStruct((2, 18, 64, 128), bf16),
            jax.ShapeDtypeStruct((2, 64, 27, 128), bf16), jax.ShapeDtypeStruct((3, 1152, 128), bf16)]
    return pl.pallas_call(
        functools.partial(forward_kernel, scale),
        grid=(2,),
        in_specs=[pl.BlockSpec(memory_space=pltpu.SMEM)] + [crop(a.shape) for a in ins] + [whole(mine.shape), whole(other.shape)],
        out_specs=[crop(outs[0].shape), crop(outs[1].shape), whole(outs[2].shape), whole(outs[3].shape)],
        out_shape=outs,
        scratch_shapes=[pltpu.VMEM((20, 64, 1152), bf16), pltpu.VMEM((3488, 128), f32), pltpu.VMEM((3, 1152, 128), bf16),
                        pltpu.VMEM((1152, 384), bf16), pltpu.VMEM((384, 1152), f32),
                        pltpu.VMEM((18, 64, 128), bf16)],
        compiler_params=pltpu.CompilerParams(vmem_limit_bytes=40 * 2**20),
        cost_estimate=pl.CostEstimate(flops=8 * 10**9, bytes_accessed=8 * 10**6, transcendentals=300000),
        name="forward",
    )(core, *ins, mine, other)


def backward_kernel(center, ylo, yhi, zlo, zhi, kern, out, windows):
    fill_windows(center, ylo, yhi, zlo, zhi, windows, 18)

    def layer(i, _):
        x = 4 * i
        grad = jnp.zeros((256, 128), f32)
        for kx in range(3):
            lhs = windows[pl.ds(x + kx, 4)].reshape(256, 1152)
            grad += jnp.dot(lhs, kern[kx], preferred_element_type=f32)
        out[0, pl.ds(x, 4)] = grad.astype(bf16).reshape(4, 64, 128)
        return 0

    lax.fori_loop(0, 4, layer, 0)


def backward(center, ylo, yhi, zlo, zhi, kern):
    def crop(shape):
        return pl.BlockSpec((1, *shape[1:]), lambda b: (b,) + (0,) * (len(shape) - 1))
    ins = (center, ylo, yhi, zlo, zhi)
    out = jax.ShapeDtypeStruct((2, 16, 64, 128), bf16)
    return pl.pallas_call(
        backward_kernel,
        grid=(2,),
        in_specs=[crop(a.shape) for a in ins] + [pl.BlockSpec(kern.shape, lambda b: (0, 0, 0), pipeline_mode=pl.Buffered(1))],
        out_specs=crop(out.shape),
        out_shape=out,
        scratch_shapes=[pltpu.VMEM((18, 64, 1152), bf16)],
        compiler_params=pltpu.CompilerParams(vmem_limit_bytes=30 * 2**20),
        cost_estimate=pl.CostEstimate(flops=4 * 10**9, bytes_accessed=3 * 10**6, transcendentals=0),
        name="backward",
    )(*ins, kern)


def flip_pairs(count, bit):
    return [(i, i ^ bit) for i in range(count)]


def odd_pairs(count, stride, length):
    pairs = []
    for i in range(count):
        coord = i // stride % length
        other = coord + 1 if coord % 2 == 1 else coord - 1
        if 0 <= other < length:
            pairs.append((i, i + (other - coord) * stride))
    return pairs


def swap_layers(first, last, coord, stride, length):
    devices = lax.axis_size("space")
    even = coord % 2 == 0
    inner = lax.ppermute(jnp.where(even, last, first), "space", flip_pairs(devices, stride))
    if length == 2:
        outer = jnp.zeros_like(inner)
    else:
        outer = lax.ppermute(
            jnp.where(even, first, last), "space", odd_pairs(devices, stride, length)
        )
    return jnp.where(even, outer, inner), jnp.where(even, inner, outer)


def core_swap(value):
    return lax.ppermute(value, "sample", flip_pairs(lax.axis_size("sample"), 1))


def chip_swap(value):
    return lax.ppermute(value, "sample", flip_pairs(lax.axis_size("sample"), 2))


def halves_joined(mine, other, core, dim):
    low = jnp.where(core == 0, mine, other)
    high = jnp.where(core == 0, other, mine)
    return jnp.concatenate([low, high], dim)


def coords():
    place = lax.axis_index("space")
    return place // (GZ * GY), place // GZ % GY, place % GZ


def side_halo(center):
    _, coord_y, coord_z = coords()
    devices = lax.axis_size("space")
    face = jnp.where(coord_y == 0, center[:, :, -1], center[:, :, 0])
    got = lax.ppermute(face, "space", flip_pairs(devices, GZ))
    none = jnp.zeros_like(got)
    ylo, yhi = jnp.where(coord_y == 0, none, got), jnp.where(coord_y == 0, got, none)
    first, last = (
        jnp.concatenate([ylo[:, :, None, at], center[:, :, :, at], yhi[:, :, None, at]], 2)
        for at in (0, center.shape[3] - 1)
    )
    zlo, zhi = swap_layers(first, last, coord_z, 1, GZ)
    return ylo, yhi, zlo, zhi


def half_kernels(rows, core):
    devices = lax.axis_size("space")
    half = rows.shape[0] // 2
    mine = lax.dynamic_slice_in_dim(rows, core * half, half, 0)
    copies = jnp.broadcast_to(mine, (devices, *mine.shape))
    got = lax.all_to_all(copies, "space", split_axis=0, concat_axis=0, tiled=True)
    return got, core_swap(got)


def own_rows_sum(parts, core):
    mine = lax.dynamic_index_in_dim(parts, core, 0, False)
    away = lax.dynamic_index_in_dim(parts, 1 - core, 0, False)
    chip = mine.astype(f32) + core_swap(away).astype(f32)
    arrived = lax.all_to_all(chip.astype(bf16), "space", split_axis=0, concat_axis=0, tiled=True)
    owned = arrived.astype(f32).sum(axis=0)
    owned = owned + chip_swap(owned)
    return halves_joined(owned, core_swap(owned), core, 0)


def local(acts, weight, moment, second, cotangent):
    field = acts[:, 0]
    grad_out = cotangent[:, 0]
    crops, nx, ny, nz, channels = field.shape
    core = lax.axis_index("sample") % 2
    coord_x = coords()[0]
    mine, other = half_kernels(weight.astype(bf16), core)
    first = jnp.concatenate([field[:, :2], grad_out[:, :1]], 1)
    last = jnp.concatenate([field[:, -2:], grad_out[:, -1:]], 1)
    groups = lax.axis_size("space") // (GY * GZ)
    below, above = swap_layers(first, last, coord_x, GY * GZ, groups)
    center = jnp.concatenate([below[:, :2], field, above[:, :2]], 1)
    dy = jnp.concatenate([below[:, 2:], grad_out, above[:, 2:]], 1)
    total = crops * lax.axis_size("sample") * lax.axis_size("space") * nx * ny * nz
    output, dz, parts, kernel = forward(
        jnp.full((1,), core, jnp.int32),
        center,
        *side_halo(center),
        dy.reshape(crops, nx + 2, ny * nz, channels),
        mine,
        other,
        float(total) ** (-0.5),
    )
    dz = dz.reshape(crops, nx + 2, ny, nz, channels)
    taps = kernel.reshape(3, 3, 3, channels, channels)
    flipped = jnp.flip(taps, (0, 1, 2)).transpose(0, 1, 2, 4, 3).reshape(kernel.shape)
    input_grad = backward(dz, *side_halo(dz), flipped)
    weight_grad = own_rows_sum(parts, core)
    new_moment = 0.9 * moment + 0.1 * weight_grad
    new_second = 0.999 * second + 0.001 * weight_grad * weight_grad
    first_fix = 1.0 - 0.9**10
    second_fix = 1.0 - 0.999**10
    new_weight = weight - 0.001 * (new_moment / first_fix) / (
        jnp.sqrt(new_second / second_fix) + 1e-08
    )
    return (
        output.reshape(acts.shape),
        input_grad.reshape(acts.shape),
        weight_grad,
        new_weight,
        new_moment,
        new_second,
    )


def solution(mesh):
    in_specs = (
        P("sample", "space", None, None, None, None),
        P("space", None),
        P("space", None),
        P("space", None),
        P("sample", "space", None, None, None, None),
    )
    out_specs = (
        P("sample", "space", None, None, None, None),
        P("sample", "space", None, None, None, None),
        P("space", None),
        P("space", None),
        P("space", None),
        P("space", None),
    )
    return jax.shard_map(local, mesh=mesh, in_specs=in_specs, out_specs=out_specs, check_vma=False)
```

```python
import functools

import jax
import jax.numpy as jnp
from jax import lax
from jax.experimental import pallas as pl
from jax.experimental.pallas import tpu as pltpu
from jax.sharding import PartitionSpec as P

GY = 2
GZ = 4

root_coef = 0.7978845608
cubic_coef = 0.044715
bf16, f32 = jnp.bfloat16, jnp.float32


def activate(pre):
    square = pre * pre
    inner = root_coef * (pre + cubic_coef * pre * square)
    tval = jnp.tanh(inner)
    value = 0.5 * pre * (1.0 + tval)
    slope = 0.5 * (1.0 + tval) + 0.5 * pre * (1.0 - tval * tval) * root_coef * (
        1.0 + 3.0 * cubic_coef * square
    )
    return (value, slope)


def fill_windows(windows, start, layers, source):
    place = lax.broadcasted_iota(jnp.int32, (8, 128), 0)

    def one(x, _):
        shifted = [[], [], []]
        for row, low, high in source(x):
            lo, hi = jnp.broadcast_to(low, (8, 128)), jnp.broadcast_to(high, (8, 128))
            shifted[0].append(jnp.where(place == 0, lo, pltpu.roll(row, 1, 0)))
            shifted[1].append(row)
            shifted[2].append(jnp.where(place == 7, hi, pltpu.roll(row, 7, 0)))
        for ky in range(3):
            for kz in range(3):
                col = (ky * 3 + kz) * 128
                tile = jnp.concatenate(shifted[kz][ky : ky + 8], axis=0).astype(bf16)
                windows[start + x, :, col : col + 128] = tile
        return 0

    lax.fori_loop(0, layers, one, 0)


def z_first_source(center, zlo, zhi, ylo, yhi, ahead=0):
    def source(x):
        at = x + ahead
        wide, low, high = (ref.astype(f32) for ref in (center[0, x], zlo[0, at], zhi[0, at]))
        below, above = ylo[0, at].astype(f32), yhi[0, at].astype(f32)
        rows = [(below[0:8], below[8:9], below[9:10])]
        rows += [(wide[8 * y : 8 * y + 8], low[y : y + 1], high[y : y + 1]) for y in range(8)]
        return rows + [(above[0:8], above[8:9], above[9:10])]

    return source


def y_first_source(center, ylo, yhi, zlo, zhi):
    def source(x):
        wide, low, high = (ref.astype(f32) for ref in (center[0, x], zlo[0, x], zhi[0, x]))
        rows = [ylo[0, x].astype(f32)] + [wide[8 * y : 8 * y + 8] for y in range(8)]
        rows += [yhi[0, x].astype(f32)]
        return [(rows[y], low[y : y + 1], high[y : y + 1]) for y in range(10)]

    return source


def forward_kernel(core_ref, center, zlo, zhi, ylo, yhi, dy, below, above, mine, other,
                   out, dz, windows_out, kern, rows, values, dys):
    step = pl.program_id(0)
    core = core_ref[0]
    windows = windows_out.at[0]

    @pl.when(step == 0)
    def _():
        def piece(s, _):
            a, b = mine[s].astype(f32), other[s].astype(f32)
            rows[pl.ds(54 * s, 27), :] = jnp.where(core == 0, a, b)
            rows[pl.ds(54 * s + 27, 27), :] = jnp.where(core == 0, b, a)
            return 0
        lax.fori_loop(0, 64, piece, 0)
        for kx in range(3):
            kern[kx] = rows[1152 * kx : 1152 * (kx + 1), :].astype(bf16)

    side = (zlo, zhi, ylo, yhi)
    fill_windows(windows, 0, 2, z_first_source(below, *side))
    fill_windows(windows, 2, 16, z_first_source(center, *side, 2))
    fill_windows(windows, 18, 2, z_first_source(above, *side, 18))
    dys[0] = below[0, 2]
    dys[1:17] = dy[0]
    dys[17] = above[0, 2]

    def layer(i, _):
        x = 3 * i
        pre = jnp.zeros((192, 128), f32)
        for kx in range(3):
            lhs = windows[pl.ds(x + kx, 3)].reshape(192, 1152)
            pre += jnp.dot(lhs, kern[kx], preferred_element_type=f32)
        value, slope = activate(pre)
        grad = (dys[pl.ds(x, 3)].reshape(192, 128).astype(f32) * slope).astype(bf16)
        dz[0, pl.ds(x, 3)] = grad.reshape(3, 64, 128)
        values[pl.ds(x, 3)] = value.astype(bf16).reshape(3, 64, 128)
        return 0

    lax.fori_loop(0, 6, layer, 0)
    out[0] = values[1:17]


def crop_block(shape):
    return pl.BlockSpec((1, *shape[1:]), lambda b: (b,) + (0,) * (len(shape) - 1))


def whole_block(shape):
    return pl.BlockSpec(shape, lambda b: (0,) * len(shape), pipeline_mode=pl.Buffered(1))


def forward(core, center, zlo, zhi, ylo, yhi, dy, below, above, mine, other):
    ins = (center, zlo, zhi, ylo, yhi, dy, below, above)
    outs = [
        jax.ShapeDtypeStruct((2, 16, 64, 128), bf16),
        jax.ShapeDtypeStruct((2, 18, 64, 128), bf16),
        jax.ShapeDtypeStruct((2, 20, 64, 1152), bf16),
        jax.ShapeDtypeStruct((3, 1152, 128), bf16),
    ]
    return pl.pallas_call(
        forward_kernel,
        grid=(2,),
        in_specs=[pl.BlockSpec(memory_space=pltpu.SMEM)]
        + [crop_block(a.shape) for a in ins]
        + [whole_block(mine.shape), whole_block(other.shape)],
        out_specs=[crop_block(o.shape) for o in outs[:3]] + [whole_block(outs[3].shape)],
        out_shape=outs,
        scratch_shapes=[
            pltpu.VMEM((3488, 128), f32),
            pltpu.VMEM((18, 64, 128), bf16),
            pltpu.VMEM((18, 64, 128), bf16),
        ],
        compiler_params=pltpu.CompilerParams(vmem_limit_bytes=24 * 2**20),
        cost_estimate=pl.CostEstimate(flops=4 * 10**9, bytes_accessed=8 * 10**6, transcendentals=300000),
        name="forward",
    )(core, *ins, mine, other)


def weight_grad_kernel(scale, core_ref, windows, dz, stays, leaves, rows, dzs, total):
    step = pl.program_id(0)
    core = core_ref[0]
    own = dz[0, 1:17].reshape(1024, 128)
    dzs[...] = jnp.zeros_like(dzs)
    for kx in range(3):
        dzs[64 * kx : 64 * kx + 1024, 128 * kx : 128 * (kx + 1)] = own
    both = windows[0, 1:19].reshape(1152, 1152)
    term = lax.dot_general(dzs[...], both, (((0,), (0,)), ((), ())), preferred_element_type=f32)

    @pl.when(step == 0)
    def _():
        total[...] = term

    @pl.when(step == 1)
    def _():
        whole = (total[...] + term) * scale
        for kx in range(3):
            for t in range(9):
                block = whole[128 * kx : 128 * (kx + 1), 128 * t : 128 * (t + 1)]
                row = (kx * 9 + t) * 128
                rows[row : row + 128, :] = block.T
        def piece(s, _):
            low, high = rows[pl.ds(54 * s, 27), :], rows[pl.ds(54 * s + 27, 27), :]
            stays[s] = jnp.where(core == 0, low, high).astype(bf16)
            leaves[s] = jnp.where(core == 0, high, low).astype(bf16)
            return 0
        lax.fori_loop(0, 64, piece, 0)


def weight_grad_halves(core, windows, dz, scale):
    half = jax.ShapeDtypeStruct((64, 27, 128), bf16)
    return pl.pallas_call(
        functools.partial(weight_grad_kernel, scale),
        grid=(2,),
        in_specs=[pl.BlockSpec(memory_space=pltpu.SMEM), crop_block(windows.shape), crop_block(dz.shape)],
        out_specs=[whole_block(half.shape)] * 2,
        out_shape=[half] * 2,
        scratch_shapes=[
            pltpu.VMEM((3488, 128), f32),
            pltpu.VMEM((1152, 384), bf16),
            pltpu.VMEM((384, 1152), f32),
        ],
        compiler_params=pltpu.CompilerParams(vmem_limit_bytes=24 * 2**20),
        cost_estimate=pl.CostEstimate(flops=4 * 10**9, bytes_accessed=7 * 10**6, transcendentals=0),
        name="weight_grad_halves",
    )(core, windows, dz)


def chip_kernel(stays, got, chip):
    chip[...] = (stays[...].astype(f32) + got[...].astype(f32)).astype(bf16)


def chip_sum(stays, got):
    vmem = pl.BlockSpec(memory_space=pltpu.VMEM)
    return pl.pallas_call(
        chip_kernel,
        in_specs=[vmem, vmem],
        out_specs=vmem,
        out_shape=jax.ShapeDtypeStruct(stays.shape, bf16),
        compiler_params=pltpu.CompilerParams(vmem_limit_bytes=4 * 2**20),
        name="chip_sum",
    )(stays, got)


def backward_kernel(center, ylo, yhi, zlo, zhi, kern, out, windows):
    fill_windows(windows, 0, 18, y_first_source(center, ylo, yhi, zlo, zhi))

    def layer(i, _):
        x = 4 * i
        grad = jnp.zeros((256, 128), f32)
        for kx in range(3):
            lhs = windows[pl.ds(x + kx, 4)].reshape(256, 1152)
            grad += jnp.dot(lhs, kern[kx], preferred_element_type=f32)
        out[0, pl.ds(x, 4)] = grad.astype(bf16).reshape(4, 64, 128)
        return 0

    lax.fori_loop(0, 4, layer, 0)


def backward(center, ylo, yhi, zlo, zhi, kern):
    def crop(shape):
        return pl.BlockSpec((1, *shape[1:]), lambda b: (b,) + (0,) * (len(shape) - 1))
    ins = (center, ylo, yhi, zlo, zhi)
    out = jax.ShapeDtypeStruct((2, 16, 64, 128), bf16)
    return pl.pallas_call(
        backward_kernel,
        grid=(2,),
        in_specs=[crop(a.shape) for a in ins] + [pl.BlockSpec(kern.shape, lambda b: (0, 0, 0), pipeline_mode=pl.Buffered(1))],
        out_specs=crop(out.shape),
        out_shape=out,
        scratch_shapes=[pltpu.VMEM((18, 64, 1152), bf16)],
        compiler_params=pltpu.CompilerParams(vmem_limit_bytes=20 * 2**20),
        cost_estimate=pl.CostEstimate(flops=4 * 10**9, bytes_accessed=3 * 10**6, transcendentals=0),
        name="backward",
    )(*ins, kern)


def flip_pairs(count, bit):
    return [(i, i ^ bit) for i in range(count)]


def odd_pairs(count, stride, length):
    pairs = []
    for i in range(count):
        coord = i // stride % length
        other = coord + 1 if coord % 2 == 1 else coord - 1
        if 0 <= other < length:
            pairs.append((i, i + (other - coord) * stride))
    return pairs


def swap_layers(first, last, coord, stride, length):
    devices = lax.axis_size("space")
    even = coord % 2 == 0
    inner = lax.ppermute(jnp.where(even, last, first), "space", flip_pairs(devices, stride))
    if length == 2:
        outer = jnp.zeros_like(inner)
    else:
        outer = lax.ppermute(
            jnp.where(even, first, last), "space", odd_pairs(devices, stride, length)
        )
    return jnp.where(even, outer, inner), jnp.where(even, inner, outer)


def core_swap(value):
    return lax.ppermute(value, "sample", flip_pairs(lax.axis_size("sample"), 1))


def chip_swap(value):
    return lax.ppermute(value, "sample", flip_pairs(lax.axis_size("sample"), 2))


def halves_joined(mine, other, core, dim):
    low = jnp.where(core == 0, mine, other)
    high = jnp.where(core == 0, other, mine)
    return jnp.concatenate([low, high], dim)


def coords():
    place = lax.axis_index("space")
    return place // (GZ * GY), place // GZ % GY, place % GZ


def y_halo(first, last, after=None):
    coord_y = coords()[1]
    face = jnp.where(coord_y == 0, last, first)
    got = lax.ppermute(face, "space", flip_pairs(lax.axis_size("space"), GZ))
    got = got if after is None else gate(got, after)
    none = jnp.zeros_like(got)
    return jnp.where(coord_y == 0, none, got), jnp.where(coord_y == 0, got, none)


def y_layers(field):
    return field[:, :, :8], field[:, :, -8:]


def z_halo(first, last):
    return swap_layers(first, last, coords()[2], 1, GZ)


def z_layers(field):
    tall = field.reshape(*field.shape[:2], 8, 8, field.shape[3])
    return tall[:, :, :, 0], tall[:, :, :, 7]


def x_halo(field, dy):
    groups = lax.axis_size("space") // (GY * GZ)
    first = jnp.concatenate([field[:, :2], dy[:, :1]], 1)
    last = jnp.concatenate([field[:, -2:], dy[:, -1:]], 1)
    return swap_layers(first, last, coords()[0], GY * GZ, groups)


def gate_kernel(value, after, same):
    pass


def gate(value, after):
    space = pl.BlockSpec(memory_space=pl.ANY)
    return pl.pallas_call(
        gate_kernel,
        in_specs=[space, space],
        out_specs=space,
        out_shape=jax.ShapeDtypeStruct(value.shape, value.dtype),
        input_output_aliases={0: 0},
        compiler_params=pltpu.CompilerParams(vmem_limit_bytes=2**20),
        name="gate",
    )(value, after)


def sum_kernel(arrived, after, total):
    total[...] = arrived[...].astype(f32).sum(axis=0)


def sum_of_arrived(arrived, after):
    return pl.pallas_call(
        sum_kernel,
        in_specs=[pl.BlockSpec(memory_space=pltpu.VMEM), pl.BlockSpec(memory_space=pl.ANY)],
        out_shape=jax.ShapeDtypeStruct(arrived.shape[1:], f32),
        compiler_params=pltpu.CompilerParams(vmem_limit_bytes=4 * 2**20),
        cost_estimate=pl.CostEstimate(flops=10**6, bytes_accessed=5 * 10**5, transcendentals=0),
        name="sum_of_arrived",
    )(arrived, after)


def half_kernels(rows, core):
    devices = lax.axis_size("space")
    half = rows.shape[0] // 2
    mine = lax.dynamic_slice_in_dim(rows, core * half, half, 0)
    copies = jnp.broadcast_to(mine, (devices, *mine.shape))
    return lax.all_to_all(copies, "space", split_axis=0, concat_axis=0, tiled=True)


def local(acts, weight, moment, second, cotangent):
    crops, _, nx, ny, nz, channels = acts.shape
    field = acts.reshape(crops, nx, ny * nz, channels)
    grad_out = cotangent.reshape(field.shape)
    core = lax.axis_index("sample") % 2
    mine = half_kernels(weight.astype(bf16), core)
    below, above = x_halo(field, grad_out)

    def along(layers):
        pairs = zip(layers(below[:, :2]), layers(field), layers(above[:, :2]))
        return [jnp.concatenate(three, 1) for three in pairs]

    zlo, zhi = z_halo(*along(z_layers))
    ylo, yhi = y_halo(
        *(
            jnp.concatenate([face, zlo[:, :, at : at + 1], zhi[:, :, at : at + 1]], 2)
            for at, face in zip((0, 7), along(y_layers))
        )
    )
    total = crops * lax.axis_size("sample") * lax.axis_size("space") * nx * ny * nz
    which = jnp.full((1,), core, jnp.int32)
    mine = gate(mine, yhi)
    other = core_swap(mine)
    output, dz, windows, kernel = forward(
        which, field, zlo, zhi, ylo, yhi, grad_out, below, above, mine, other
    )
    stays, leaves = weight_grad_halves(which, windows, dz, float(total) ** (-0.5))
    chip = chip_sum(stays, core_swap(leaves))
    ylo, yhi = y_halo(*y_layers(dz), chip)
    zlo, zhi = z_halo(
        *(
            jnp.concatenate([ylo[:, :, at : at + 1], face, yhi[:, :, at : at + 1]], 2)
            for at, face in zip((0, 7), z_layers(dz))
        )
    )
    arrived = lax.all_to_all(chip, "space", split_axis=0, concat_axis=0, tiled=True)
    taps = kernel.reshape(3, 3, 3, channels, channels)
    flipped = jnp.flip(taps, (0, 1, 2)).transpose(0, 1, 2, 4, 3).reshape(kernel.shape)
    input_grad = backward(dz, ylo, yhi, zlo, zhi, flipped)
    owned = sum_of_arrived(arrived, input_grad)
    owned = owned + chip_swap(owned)
    weight_grad = halves_joined(owned, core_swap(owned), core, 0)
    new_moment = 0.9 * moment + 0.1 * weight_grad
    new_second = 0.999 * second + 0.001 * weight_grad * weight_grad
    first_fix = 1.0 - 0.9**10
    second_fix = 1.0 - 0.999**10
    new_weight = weight - 0.001 * (new_moment / first_fix) / (
        jnp.sqrt(new_second / second_fix) + 1e-08
    )
    return (
        output.reshape(acts.shape),
        input_grad.reshape(acts.shape),
        weight_grad,
        new_weight,
        new_moment,
        new_second,
    )


def solution(mesh):
    in_specs = (
        P("sample", "space", None, None, None, None),
        P("space", None),
        P("space", None),
        P("space", None),
        P("sample", "space", None, None, None, None),
    )
    out_specs = (
        P("sample", "space", None, None, None, None),
        P("sample", "space", None, None, None, None),
        P("space", None),
        P("space", None),
        P("space", None),
        P("space", None),
    )
    return jax.shard_map(local, mesh=mesh, in_specs=in_specs, out_specs=out_specs, check_vma=False)
```

```python
import functools

import jax
import jax.numpy as jnp
from jax import lax
from jax.experimental import pallas as pl
from jax.experimental.pallas import tpu as pltpu
from jax.sharding import PartitionSpec as P

GY = 2
GZ = 4
FWD_VMEM = 20

root_coef = 0.7978845608
cubic_coef = 0.044715
bf16, f32 = jnp.bfloat16, jnp.float32


def activate(pre):
    square = pre * pre
    inner = root_coef * (pre + cubic_coef * pre * square)
    tval = jnp.tanh(inner)
    value = 0.5 * pre * (1.0 + tval)
    slope = 0.5 * (1.0 + tval) + 0.5 * pre * (1.0 - tval * tval) * root_coef * (
        1.0 + 3.0 * cubic_coef * square
    )
    return (value, slope)


def fill_windows(windows, start, layers, source):
    place = lax.broadcasted_iota(jnp.int32, (8, 128), 0)

    def one(x, _):
        at = start + x
        shifted = [[], [], []]
        for row, low, high in source(x):
            lo, hi = jnp.broadcast_to(low, (8, 128)), jnp.broadcast_to(high, (8, 128))
            shifted[0].append(jnp.where(place == 0, lo, pltpu.roll(row, 1, 0)))
            shifted[1].append(row)
            shifted[2].append(jnp.where(place == 7, hi, pltpu.roll(row, 7, 0)))
        for ky in range(3):
            for kz in range(3):
                col = (ky * 3 + kz) * 128
                tile = jnp.concatenate(shifted[kz][ky : ky + 8], axis=0).astype(bf16)
                windows[lax.div(at, 2), lax.rem(at, 2), :, col : col + 128] = tile
        return 0

    lax.fori_loop(0, layers, one, 0)


def z_first_source(b, center, zlo, zhi, ylo, yhi, ahead=0):
    def source(x):
        at = x + ahead
        wide, low, high = (ref.astype(f32) for ref in (center[b, x], zlo[b, at], zhi[b, at]))
        below, above = ylo[b, at].astype(f32), yhi[b, at].astype(f32)
        rows = [(below[0:8], below[8:9], below[9:10])]
        rows += [(wide[8 * y : 8 * y + 8], low[y : y + 1], high[y : y + 1]) for y in range(8)]
        return rows + [(above[0:8], above[8:9], above[9:10])]

    return source


def y_first_source(b, center, ylo, yhi, zlo, zhi):
    def source(x):
        wide, low, high = (ref.astype(f32) for ref in (center[b, x], zlo[b, x], zhi[b, x]))
        rows = [ylo[b, x].astype(f32)] + [wide[8 * y : 8 * y + 8] for y in range(8)]
        rows += [yhi[b, x].astype(f32)]
        return [(rows[y], low[y : y + 1], high[y : y + 1]) for y in range(10)]

    return source


def pair_kernels(kern, wide):
    none = jnp.zeros((1152, 128), bf16)
    for at in range(4):
        wide[at, :, 0:128] = kern[at] if at < 3 else none
        wide[at, :, 128:256] = kern[at - 1] if at > 0 else none


def pair_products(windows, wide, pairs):
    total = jnp.zeros((64 * pairs, 256), f32)
    for at in range(4):
        lhs = windows[at // 2 : at // 2 + pairs, at % 2].reshape(64 * pairs, 1152)
        total += jnp.dot(lhs, wide[at], preferred_element_type=f32)
    return total


def forward_kernel(core_ref, center, zlo, zhi, ylo, yhi, dy, below, above, mine, other,
                   out, dz, windows, kern, rows, wide):
    core = core_ref[0]

    def piece(s, _):
        a, b = mine[s].astype(f32), other[s].astype(f32)
        rows[pl.ds(54 * s, 27), :] = jnp.where(core == 0, a, b)
        rows[pl.ds(54 * s + 27, 27), :] = jnp.where(core == 0, b, a)
        return 0

    lax.fori_loop(0, 64, piece, 0)
    for kx in range(3):
        kern[kx] = rows[1152 * kx : 1152 * (kx + 1), :].astype(bf16)
    pair_kernels(kern, wide)
    side = (zlo, zhi, ylo, yhi)

    def crop(b, _):
        own = windows.at[b]
        fill_windows(own, 0, 2, z_first_source(b, below, *side))
        fill_windows(own, 2, 16, z_first_source(b, center, *side, 2))
        fill_windows(own, 18, 2, z_first_source(b, above, *side, 18))
        both = pair_products(own, wide, 9)
        for at in range(2):
            value, slope = activate(both[:, 128 * at : 128 * (at + 1)])
            grad = dy[b, :, at].reshape(576, 128).astype(f32) * slope
            dz[b, :, at] = grad.astype(bf16).reshape(9, 64, 128)
            value = value.astype(bf16).reshape(9, 64, 128)
            out[b, :, 1 - at] = value[1:9] if at == 0 else value[0:8]
        return 0

    lax.fori_loop(0, 2, crop, 0)


VMEM = pl.BlockSpec(memory_space=pltpu.VMEM)
SMEM = pl.BlockSpec(memory_space=pltpu.SMEM)
ANY = pl.BlockSpec(memory_space=pl.ANY)


def forward(core, center, zlo, zhi, ylo, yhi, dy, below, above, mine, other):
    ins = (center, zlo, zhi, ylo, yhi, dy.reshape(2, 9, 2, 64, 128), below, above, mine, other)
    outs = [
        jax.ShapeDtypeStruct((2, 8, 2, 64, 128), bf16),
        jax.ShapeDtypeStruct((2, 9, 2, 64, 128), bf16),
        jax.ShapeDtypeStruct((2, 10, 2, 64, 1152), bf16),
        jax.ShapeDtypeStruct((3, 1152, 128), bf16),
    ]
    out, dz, windows, kern = pl.pallas_call(
        forward_kernel,
        in_specs=[SMEM] + [VMEM] * len(ins),
        out_specs=[VMEM] * 4,
        out_shape=outs,
        scratch_shapes=[pltpu.VMEM((3488, 128), f32), pltpu.VMEM((4, 1152, 256), bf16)],
        compiler_params=pltpu.CompilerParams(vmem_limit_bytes=FWD_VMEM * 2**20),
        cost_estimate=pl.CostEstimate(flops=4 * 10**9, bytes_accessed=8 * 10**6, transcendentals=300000),
        name="forward",
    )(core, *ins)
    return out, dz.reshape(2, 18, 64, 128), windows.reshape(2, 20, 64, 1152), kern


def weight_grad_kernel(scale, core_ref, windows, dz, stays, leaves, rows, dzs, total):
    core = core_ref[0]
    dzs[...] = jnp.zeros_like(dzs)
    for b in range(2):
        own = dz[b, 1:17].reshape(1024, 128)
        for kx in range(3):
            dzs[64 * kx : 64 * kx + 1024, 128 * kx : 128 * (kx + 1)] = own
        both = windows[b, 1:19].reshape(1152, 1152)
        term = lax.dot_general(dzs[...], both, (((0,), (0,)), ((), ())), preferred_element_type=f32)
        if b == 0:
            total[...] = term
    whole = (total[...] + term) * scale
    for kx in range(3):
        for t in range(9):
            block = whole[128 * kx : 128 * (kx + 1), 128 * t : 128 * (t + 1)]
            row = (kx * 9 + t) * 128
            rows[row : row + 128, :] = block.T

    def piece(s, _):
        low, high = rows[pl.ds(54 * s, 27), :], rows[pl.ds(54 * s + 27, 27), :]
        stays[s] = jnp.where(core == 0, low, high).astype(bf16)
        leaves[s] = jnp.where(core == 0, high, low).astype(bf16)
        return 0

    lax.fori_loop(0, 64, piece, 0)


def weight_grad_halves(core, windows, dz, scale):
    half = jax.ShapeDtypeStruct((64, 27, 128), bf16)
    return pl.pallas_call(
        functools.partial(weight_grad_kernel, scale),
        in_specs=[SMEM, VMEM, VMEM],
        out_specs=[VMEM] * 2,
        out_shape=[half] * 2,
        scratch_shapes=[
            pltpu.VMEM((3488, 128), f32),
            pltpu.VMEM((1152, 384), bf16),
            pltpu.VMEM((384, 1152), f32),
        ],
        compiler_params=pltpu.CompilerParams(vmem_limit_bytes=FWD_VMEM * 2**20),
        cost_estimate=pl.CostEstimate(flops=4 * 10**9, bytes_accessed=7 * 10**6, transcendentals=0),
        name="weight_grad_halves",
    )(core, windows, dz)


def chip_kernel(stays, got, chip):
    chip[...] = (stays[...].astype(f32) + got[...].astype(f32)).astype(bf16)


def chip_sum(stays, got):
    vmem = pl.BlockSpec(memory_space=pltpu.VMEM)
    return pl.pallas_call(
        chip_kernel,
        in_specs=[vmem, vmem],
        out_specs=vmem,
        out_shape=jax.ShapeDtypeStruct(stays.shape, bf16),
        compiler_params=pltpu.CompilerParams(vmem_limit_bytes=4 * 2**20),
        name="chip_sum",
    )(stays, got)


def backward_kernel(center, ylo, yhi, zlo, zhi, kern, out, token, windows, wide):
    token[...] = jnp.zeros_like(token)
    pair_kernels(kern, wide)

    def crop(b, _):
        fill_windows(windows, 0, 18, y_first_source(b, center, ylo, yhi, zlo, zhi))
        both = pair_products(windows, wide, 8).astype(bf16)
        for at in range(2):
            out[b, :, at] = both[:, 128 * at : 128 * (at + 1)].reshape(8, 64, 128)
        return 0

    lax.fori_loop(0, 2, crop, 0)


def backward(center, ylo, yhi, zlo, zhi, kern):
    return pl.pallas_call(
        backward_kernel,
        in_specs=[VMEM] * 6,
        out_specs=[VMEM] * 2,
        out_shape=[jax.ShapeDtypeStruct((2, 8, 2, 64, 128), bf16), jax.ShapeDtypeStruct((8, 128), f32)],
        scratch_shapes=[pltpu.VMEM((9, 2, 64, 1152), bf16), pltpu.VMEM((4, 1152, 256), bf16)],
        compiler_params=pltpu.CompilerParams(vmem_limit_bytes=FWD_VMEM * 2**20),
        cost_estimate=pl.CostEstimate(flops=4 * 10**9, bytes_accessed=3 * 10**6, transcendentals=0),
        name="backward",
    )(center, ylo, yhi, zlo, zhi, kern)


def flip_pairs(count, bit):
    return [(i, i ^ bit) for i in range(count)]


def odd_pairs(count, stride, length):
    pairs = []
    for i in range(count):
        coord = i // stride % length
        other = coord + 1 if coord % 2 == 1 else coord - 1
        if 0 <= other < length:
            pairs.append((i, i + (other - coord) * stride))
    return pairs


def swapped(inner, outer, even, stride, length):
    devices = lax.axis_size("space")
    inner = lax.ppermute(inner, "space", flip_pairs(devices, stride))
    outer = lax.ppermute(outer, "space", odd_pairs(devices, stride, length))
    return jnp.where(even, outer, inner), jnp.where(even, inner, outer)


def swap_layers(first, last, coord, stride, length):
    even = coord % 2 == 0
    return swapped(jnp.where(even, last, first), jnp.where(even, first, last), even, stride, length)


def core_swap(value):
    return lax.ppermute(value, "sample", flip_pairs(lax.axis_size("sample"), 1))


def chip_swap(value):
    return lax.ppermute(value, "sample", flip_pairs(lax.axis_size("sample"), 2))


def halves_joined(mine, other, core, dim):
    low = jnp.where(core == 0, mine, other)
    high = jnp.where(core == 0, other, mine)
    return jnp.concatenate([low, high], dim)


def coords():
    place = lax.axis_index("space")
    return place // (GZ * GY), place // GZ % GY, place % GZ


def y_halo(first, last, after=None):
    coord_y = coords()[1]
    face = jnp.where(coord_y == 0, last, first)
    got = lax.ppermute(face, "space", flip_pairs(lax.axis_size("space"), GZ))
    got = got if after is None else gate(got, after)
    none = jnp.zeros_like(got)
    return jnp.where(coord_y == 0, none, got), jnp.where(coord_y == 0, got, none)


def y_layers(field):
    return field[:, :, :8], field[:, :, -8:]


def z_halo(first, last):
    return swap_layers(first, last, coords()[2], 1, GZ)


def start_kernel(even_ref, core_ref, field, dy, weight, inner, outer, copies, ends, rows, wide, sems):
    def spread(at):
        return pltpu.make_async_copy(wide, copies.at[pl.ds(8 * at, 8)], sems.at[6 + at])

    fetches = [pltpu.make_async_copy(weight, rows, sems.at[0])]
    for at, x in ((0, 0), (1, 14)):
        fetches.append(pltpu.make_async_copy(field.at[:, x : x + 2], ends.at[at, :, 0:2], sems.at[1 + 2 * at]))
        x = 15 * at
        fetches.append(pltpu.make_async_copy(dy.at[:, x : x + 1], ends.at[at, :, 2:3], sems.at[2 + 2 * at]))
    for fetch in fetches:
        fetch.start()
    even, core = even_ref[0] == 1, core_ref[0]
    fetches[0].wait()
    half = jnp.where(core == 0, rows[0:27], rows[27:54]).astype(bf16)
    for at in range(8):
        wide[at] = half
    for at in range(8):
        spread(at).start()
    for fetch in fetches[1:]:
        fetch.wait()
    inner[...] = jnp.where(even, ends[1], ends[0])
    outer[...] = jnp.where(even, ends[0], ends[1])
    for at in range(8):
        spread(at).wait()


def start(even, core, field, dy, weight):
    end = jax.ShapeDtypeStruct((2, 3, 64, 128), bf16)
    return pl.pallas_call(
        start_kernel,
        in_specs=[SMEM, SMEM, ANY, ANY, ANY],
        out_specs=[VMEM, VMEM, ANY],
        out_shape=[end, end, jax.ShapeDtypeStruct((64, 27, 128), bf16)],
        scratch_shapes=[
            pltpu.VMEM((2, 2, 3, 64, 128), bf16),
            pltpu.VMEM((54, 128), f32),
            pltpu.VMEM((8, 27, 128), bf16),
            pltpu.SemaphoreType.DMA((14,)),
        ],
        name="start",
    )(even, core, field, dy, weight)


def z_edges_kernel(field, first, last, tall):
    def one(i, _):
        b, x = lax.div(i, 16), lax.rem(i, 16)
        tall[i] = field[b, x].astype(f32)
        first[b, x] = tall[i, pl.ds(0, 8, stride=8)].astype(bf16)
        last[b, x] = tall[i, pl.ds(7, 8, stride=8)].astype(bf16)
        return 0

    lax.fori_loop(0, 32, one, 0, unroll=4)


def z_edges(field):
    edge = jax.ShapeDtypeStruct((2, 16, 8, 128), bf16)
    return pl.pallas_call(
        z_edges_kernel,
        in_specs=[VMEM],
        out_specs=[VMEM] * 2,
        out_shape=[edge] * 2,
        scratch_shapes=[pltpu.VMEM((32, 64, 128), f32)],
        compiler_params=pltpu.CompilerParams(vmem_limit_bytes=4 * 2**20),
        name="z_edges",
    )(field)


def z_layers(field):
    tall = field.reshape(*field.shape[:2], 8, 8, field.shape[3])
    return tall[:, :, :, 0], tall[:, :, :, 7]


def gate_kernel(value, after, same):
    pass


def gate(value, after):
    space = pl.BlockSpec(memory_space=pl.ANY)
    return pl.pallas_call(
        gate_kernel,
        in_specs=[space, space],
        out_specs=space,
        out_shape=jax.ShapeDtypeStruct(value.shape, value.dtype),
        input_output_aliases={0: 0},
        compiler_params=pltpu.CompilerParams(vmem_limit_bytes=2**20),
        name="gate",
    )(value, after)


def sum_kernel(arrived, after, total):
    total[...] = arrived[...].astype(f32).sum(axis=0)


def sum_of_arrived(arrived, after):
    return pl.pallas_call(
        sum_kernel,
        in_specs=[pl.BlockSpec(memory_space=pltpu.VMEM), pl.BlockSpec(memory_space=pl.ANY)],
        out_shape=jax.ShapeDtypeStruct(arrived.shape[1:], f32),
        compiler_params=pltpu.CompilerParams(vmem_limit_bytes=4 * 2**20),
        cost_estimate=pl.CostEstimate(flops=10**6, bytes_accessed=5 * 10**5, transcendentals=0),
        name="sum_of_arrived",
    )(arrived, after)


def local(acts, weight, moment, second, cotangent):
    crops, _, nx, ny, nz, channels = acts.shape
    field = acts.reshape(crops, nx, ny * nz, channels)
    grad_out = cotangent.reshape(field.shape)
    core = lax.axis_index("sample") % 2
    even = coords()[0] % 2 == 0
    groups = lax.axis_size("space") // (GY * GZ)
    which = jnp.full((1,), core, jnp.int32)
    inner, outer, copies = start(jnp.full((1,), even, jnp.int32), which, field, grad_out, weight)
    mine = lax.all_to_all(copies, "space", split_axis=0, concat_axis=0, tiled=True)
    below, above = swapped(inner, outer, even, GY * GZ, groups)

    def along(layers, own):
        pairs = zip(layers(below[:, :2]), own(field), layers(above[:, :2]))
        return [jnp.concatenate(three, 1) for three in pairs]

    zlo, zhi = z_halo(*along(z_layers, z_edges))
    ylo, yhi = y_halo(
        *(
            jnp.concatenate([face, zlo[:, :, at : at + 1], zhi[:, :, at : at + 1]], 2)
            for at, face in zip((0, 7), along(y_layers, y_layers))
        )
    )
    total = crops * lax.axis_size("sample") * lax.axis_size("space") * nx * ny * nz
    mine = gate(mine, yhi)
    dy = jnp.concatenate([below[:, 2:], grad_out, above[:, 2:]], 1)
    other = core_swap(mine)
    output, dz, windows, kernel = forward(
        which, field, zlo, zhi, ylo, yhi, dy, below, above, mine, other
    )
    stays, leaves = weight_grad_halves(which, windows, dz, float(total) ** (-0.5))
    chip = chip_sum(stays, core_swap(leaves))
    ylo, yhi = y_halo(*y_layers(dz), chip)
    zlo, zhi = z_halo(
        *(
            jnp.concatenate([ylo[:, :, at : at + 1], face, yhi[:, :, at : at + 1]], 2)
            for at, face in zip((0, 7), z_layers(dz))
        )
    )
    arrived = lax.all_to_all(chip, "space", split_axis=0, concat_axis=0, tiled=True)
    taps = kernel.reshape(3, 3, 3, channels, channels)
    flipped = jnp.flip(taps, (0, 1, 2)).transpose(0, 1, 2, 4, 3).reshape(kernel.shape)
    input_grad, token = backward(dz, ylo, yhi, zlo, zhi, flipped)
    owned = sum_of_arrived(arrived, token)
    owned = owned + chip_swap(owned)
    weight_grad = halves_joined(owned, core_swap(owned), core, 0)
    new_moment = 0.9 * moment + 0.1 * weight_grad
    new_second = 0.999 * second + 0.001 * weight_grad * weight_grad
    first_fix = 1.0 - 0.9**10
    second_fix = 1.0 - 0.999**10
    new_weight = weight - 0.001 * (new_moment / first_fix) / (
        jnp.sqrt(new_second / second_fix) + 1e-08
    )
    return (
        output.reshape(acts.shape),
        input_grad.reshape(acts.shape),
        weight_grad,
        new_weight,
        new_moment,
        new_second,
    )


def solution(mesh):
    in_specs = (
        P("sample", "space", None, None, None, None),
        P("space", None),
        P("space", None),
        P("space", None),
        P("sample", "space", None, None, None, None),
    )
    out_specs = (
        P("sample", "space", None, None, None, None),
        P("sample", "space", None, None, None, None),
        P("space", None),
        P("space", None),
        P("space", None),
        P("space", None),
    )
    return jax.shard_map(local, mesh=mesh, in_specs=in_specs, out_specs=out_specs, check_vma=False)
```

```python
import functools

import jax
import jax.numpy as jnp
from jax import lax
from jax.experimental import pallas as pl
from jax.experimental.pallas import tpu as pltpu
from jax.sharding import PartitionSpec as P

GY = 2
GZ = 4
FWD_VMEM = 20
QUARTERS = (0, 27, 13, 40)

root_coef = 0.7978845608
cubic_coef = 0.044715
bf16, f32 = jnp.bfloat16, jnp.float32


def activate(pre):
    square = pre * pre
    inner = root_coef * (pre + cubic_coef * pre * square)
    tval = jnp.tanh(inner)
    value = 0.5 * pre * (1.0 + tval)
    slope = 0.5 * (1.0 + tval) + 0.5 * pre * (1.0 - tval * tval) * root_coef * (
        1.0 + 3.0 * cubic_coef * square
    )
    return (value, slope)


def fill_windows(windows, start, layers, source):
    place = lax.broadcasted_iota(jnp.int32, (8, 128), 0)

    def one(x, _):
        at = start + x
        shifted = [[], [], []]
        for row, low, high in source(x):
            lo, hi = jnp.broadcast_to(low, (8, 128)), jnp.broadcast_to(high, (8, 128))
            shifted[0].append(jnp.where(place == 0, lo, pltpu.roll(row, 1, 0)))
            shifted[1].append(row)
            shifted[2].append(jnp.where(place == 7, hi, pltpu.roll(row, 7, 0)))
        for ky in range(3):
            for kz in range(3):
                col = (ky * 3 + kz) * 128
                tile = jnp.concatenate(shifted[kz][ky : ky + 8], axis=0).astype(bf16)
                windows[lax.div(at, 2), lax.rem(at, 2), :, col : col + 128] = tile
        return 0

    lax.fori_loop(0, layers, one, 0)


def z_first_source(b, center, zlo, zhi, ylo, yhi, ahead=0):
    def source(x):
        at = x + ahead
        wide, low, high = (ref.astype(f32) for ref in (center[b, x], zlo[b, at], zhi[b, at]))
        below, above = ylo[b, at].astype(f32), yhi[b, at].astype(f32)
        rows = [(below[0:8], below[8:9], below[9:10])]
        rows += [(wide[8 * y : 8 * y + 8], low[y : y + 1], high[y : y + 1]) for y in range(8)]
        return rows + [(above[0:8], above[8:9], above[9:10])]

    return source


def y_first_source(b, center, ylo, yhi, zlo, zhi):
    def source(x):
        wide, low, high = (ref.astype(f32) for ref in (center[b, x], zlo[b, x], zhi[b, x]))
        rows = [ylo[b, x].astype(f32)] + [wide[8 * y : 8 * y + 8] for y in range(8)]
        rows += [yhi[b, x].astype(f32)]
        return [(rows[y], low[y : y + 1], high[y : y + 1]) for y in range(10)]

    return source


def pair_kernels(kern, wide):
    none = jnp.zeros((1152, 128), bf16)
    for at in range(4):
        wide[at, :, 0:128] = kern[at] if at < 3 else none
        wide[at, :, 128:256] = kern[at - 1] if at > 0 else none


def pair_products(windows, wide, pairs):
    total = jnp.zeros((64 * pairs, 256), f32)
    for at in range(4):
        lhs = windows[at // 2 : at // 2 + pairs, at % 2].reshape(64 * pairs, 1152)
        total += jnp.dot(lhs, wide[at], preferred_element_type=f32)
    return total


def forward_kernel(member_ref, center, zlo, zhi, ylo, yhi, dy, below, above, own, chip, core, slant,
                   out, dz, windows, kern, rows, wide):
    member = member_ref[0]
    side, half = lax.div(member, 2), lax.rem(member, 2)
    near, far = 27 * half, 27 - 27 * half
    starts = (near + 13 * side, near + 13 - 13 * side, far + 13 * side, far + 13 - 13 * side)

    def piece(s, _):
        for quarter, first in zip((own, chip, core, slant), starts):
            rows[pl.ds(54 * s + first, 14), :] = quarter[s].astype(f32)
        return 0

    lax.fori_loop(0, 64, piece, 0)
    for kx in range(3):
        kern[kx] = rows[1152 * kx : 1152 * (kx + 1), :].astype(bf16)
    pair_kernels(kern, wide)
    halo = (zlo, zhi, ylo, yhi)

    def crop(b, _):
        here = windows.at[b]
        fill_windows(here, 0, 2, z_first_source(b, below, *halo))
        fill_windows(here, 2, 16, z_first_source(b, center, *halo, 2))
        fill_windows(here, 18, 2, z_first_source(b, above, *halo, 18))
        both = pair_products(here, wide, 9)
        for at in range(2):
            value, slope = activate(both[:, 128 * at : 128 * (at + 1)])
            grad = dy[b, :, at].reshape(576, 128).astype(f32) * slope
            dz[b, :, at] = grad.astype(bf16).reshape(9, 64, 128)
            value = value.astype(bf16).reshape(9, 64, 128)
            out[b, :, 1 - at] = value[1:9] if at == 0 else value[0:8]
        return 0

    lax.fori_loop(0, 2, crop, 0)


VMEM = pl.BlockSpec(memory_space=pltpu.VMEM)
SMEM = pl.BlockSpec(memory_space=pltpu.SMEM)
ANY = pl.BlockSpec(memory_space=pl.ANY)


def forward(member, center, zlo, zhi, ylo, yhi, dy, below, above, quarters):
    ins = (center, zlo, zhi, ylo, yhi, dy.reshape(2, 9, 2, 64, 128), below, above, *quarters)
    outs = [
        jax.ShapeDtypeStruct((2, 8, 2, 64, 128), bf16),
        jax.ShapeDtypeStruct((2, 9, 2, 64, 128), bf16),
        jax.ShapeDtypeStruct((2, 10, 2, 64, 1152), bf16),
        jax.ShapeDtypeStruct((3, 1152, 128), bf16),
    ]
    out, dz, windows, kern = pl.pallas_call(
        forward_kernel,
        in_specs=[SMEM] + [VMEM] * len(ins),
        out_specs=[VMEM] * 4,
        out_shape=outs,
        scratch_shapes=[pltpu.VMEM((3488, 128), f32), pltpu.VMEM((4, 1152, 256), bf16)],
        compiler_params=pltpu.CompilerParams(vmem_limit_bytes=FWD_VMEM * 2**20),
        cost_estimate=pl.CostEstimate(flops=4 * 10**9, bytes_accessed=8 * 10**6, transcendentals=300000),
        name="forward",
    )(member, *ins)
    return out, dz.reshape(2, 18, 64, 128), windows.reshape(2, 20, 64, 1152), kern


def weight_grad_kernel(scale, core_ref, windows, dz, stays, leaves, rows, dzs, total):
    core = core_ref[0]
    dzs[...] = jnp.zeros_like(dzs)
    for b in range(2):
        own = dz[b, 1:17].reshape(1024, 128)
        for kx in range(3):
            dzs[64 * kx : 64 * kx + 1024, 128 * kx : 128 * (kx + 1)] = own
        both = windows[b, 1:19].reshape(1152, 1152)
        term = lax.dot_general(dzs[...], both, (((0,), (0,)), ((), ())), preferred_element_type=f32)
        if b == 0:
            total[...] = term
    whole = (total[...] + term) * scale
    for kx in range(3):
        for t in range(9):
            block = whole[128 * kx : 128 * (kx + 1), 128 * t : 128 * (t + 1)]
            row = (kx * 9 + t) * 128
            rows[row : row + 128, :] = block.T

    def piece(s, _):
        low, high = rows[pl.ds(54 * s, 27), :], rows[pl.ds(54 * s + 27, 27), :]
        stays[s] = jnp.where(core == 0, low, high).astype(bf16)
        leaves[s] = jnp.where(core == 0, high, low).astype(bf16)
        return 0

    lax.fori_loop(0, 64, piece, 0)


def weight_grad_halves(core, windows, dz, scale):
    half = jax.ShapeDtypeStruct((64, 27, 128), bf16)
    return pl.pallas_call(
        functools.partial(weight_grad_kernel, scale),
        in_specs=[SMEM, VMEM, VMEM],
        out_specs=[VMEM] * 2,
        out_shape=[half] * 2,
        scratch_shapes=[
            pltpu.VMEM((3488, 128), f32),
            pltpu.VMEM((1152, 384), bf16),
            pltpu.VMEM((384, 1152), f32),
        ],
        compiler_params=pltpu.CompilerParams(vmem_limit_bytes=FWD_VMEM * 2**20),
        cost_estimate=pl.CostEstimate(flops=4 * 10**9, bytes_accessed=7 * 10**6, transcendentals=0),
        name="weight_grad_halves",
    )(core, windows, dz)


def chip_kernel(stays, got, chip):
    chip[...] = (stays[...].astype(f32) + got[...].astype(f32)).astype(bf16)


def chip_sum(stays, got):
    vmem = pl.BlockSpec(memory_space=pltpu.VMEM)
    return pl.pallas_call(
        chip_kernel,
        in_specs=[vmem, vmem],
        out_specs=vmem,
        out_shape=jax.ShapeDtypeStruct(stays.shape, bf16),
        compiler_params=pltpu.CompilerParams(vmem_limit_bytes=4 * 2**20),
        name="chip_sum",
    )(stays, got)


def flipped_pair_kernels(kern, wide):
    none = jnp.zeros((128, 1152), bf16)
    for at in range(4):
        for side, kx in ((0, 2 - at), (1, 3 - at)):
            if not 0 <= kx <= 2:
                wide[at, 128 * side : 128 * (side + 1), :] = none
                continue
            for tap in range(9):
                col = 128 * (8 - tap)
                block = kern[kx, 128 * tap : 128 * (tap + 1), :]
                wide[at, 128 * side : 128 * (side + 1), col : col + 128] = block


def backward_kernel(center, ylo, yhi, zlo, zhi, kern, out, token, windows, wide):
    token[...] = jnp.zeros_like(token)
    flipped_pair_kernels(kern, wide)

    def crop(b, _):
        fill_windows(windows, 0, 18, y_first_source(b, center, ylo, yhi, zlo, zhi))
        both = jnp.zeros((512, 256), f32)
        for at in range(4):
            lhs = windows[at // 2 : at // 2 + 8, at % 2].reshape(512, 1152)
            both += lax.dot_general(lhs, wide[at], (((1,), (1,)), ((), ())), preferred_element_type=f32)
        for side in range(2):
            grad = both[:, 128 * side : 128 * (side + 1)].astype(bf16)
            out[b, :, side] = grad.reshape(8, 64, 128)
        return 0

    lax.fori_loop(0, 2, crop, 0)


def backward(center, ylo, yhi, zlo, zhi, kern):
    return pl.pallas_call(
        backward_kernel,
        in_specs=[VMEM] * 6,
        out_specs=[VMEM] * 2,
        out_shape=[jax.ShapeDtypeStruct((2, 8, 2, 64, 128), bf16), jax.ShapeDtypeStruct((8, 128), f32)],
        scratch_shapes=[pltpu.VMEM((9, 2, 64, 1152), bf16), pltpu.VMEM((4, 256, 1152), bf16)],
        compiler_params=pltpu.CompilerParams(vmem_limit_bytes=FWD_VMEM * 2**20),
        cost_estimate=pl.CostEstimate(flops=4 * 10**9, bytes_accessed=3 * 10**6, transcendentals=0),
        name="backward",
    )(center, ylo, yhi, zlo, zhi, kern)


def flip_pairs(count, bit):
    return [(i, i ^ bit) for i in range(count)]


def odd_pairs(count, stride, length):
    pairs = []
    for i in range(count):
        coord = i // stride % length
        other = coord + 1 if coord % 2 == 1 else coord - 1
        if 0 <= other < length:
            pairs.append((i, i + (other - coord) * stride))
    return pairs


def swapped(inner, outer, even, stride, length):
    devices = lax.axis_size("space")
    inner = lax.ppermute(inner, "space", flip_pairs(devices, stride))
    outer = lax.ppermute(outer, "space", odd_pairs(devices, stride, length))
    return jnp.where(even, outer, inner), jnp.where(even, inner, outer)


def swap_layers(first, last, coord, stride, length):
    even = coord % 2 == 0
    return swapped(jnp.where(even, last, first), jnp.where(even, first, last), even, stride, length)


def core_swap(value):
    return lax.ppermute(value, "sample", flip_pairs(lax.axis_size("sample"), 1))


def chip_swap(value):
    return lax.ppermute(value, "sample", flip_pairs(lax.axis_size("sample"), 2))


def diagonal_swap(value):
    return lax.ppermute(value, "sample", flip_pairs(lax.axis_size("sample"), 3))


def halves_joined(mine, other, core, dim):
    low = jnp.where(core == 0, mine, other)
    high = jnp.where(core == 0, other, mine)
    return jnp.concatenate([low, high], dim)


def coords():
    place = lax.axis_index("space")
    return place // (GZ * GY), place // GZ % GY, place % GZ


def y_halo(first, last, after=None):
    coord_y = coords()[1]
    face = jnp.where(coord_y == 0, last, first)
    got = lax.ppermute(face, "space", flip_pairs(lax.axis_size("space"), GZ))
    got = got if after is None else gate(got, after)
    none = jnp.zeros_like(got)
    return jnp.where(coord_y == 0, none, got), jnp.where(coord_y == 0, got, none)


def y_layers(field):
    return field[:, :, :8], field[:, :, -8:]


def z_halo(first, last):
    return swap_layers(first, last, coords()[2], 1, GZ)


def start_kernel(even_ref, member_ref, field, dy, weight, inner, outer, copies, ends, rows, wide, sems):
    def spread(at):
        return pltpu.make_async_copy(wide, copies.at[pl.ds(8 * at, 8)], sems.at[6 + at])

    fetches = [pltpu.make_async_copy(weight, rows, sems.at[0])]
    for at, x in ((0, 0), (1, 14)):
        fetches.append(pltpu.make_async_copy(field.at[:, x : x + 2], ends.at[at, :, 0:2], sems.at[1 + 2 * at]))
        x = 15 * at
        fetches.append(pltpu.make_async_copy(dy.at[:, x : x + 1], ends.at[at, :, 2:3], sems.at[2 + 2 * at]))
    for fetch in fetches:
        fetch.start()
    even, member = even_ref[0] == 1, member_ref[0]
    fetches[0].wait()
    share = rows[0:14]
    for at in range(1, 4):
        share = jnp.where(member == at, rows[QUARTERS[at] : QUARTERS[at] + 14], share)
    for at in range(8):
        wide[at] = share.astype(bf16)
    for at in range(8):
        spread(at).start()
    for fetch in fetches[1:]:
        fetch.wait()
    inner[...] = jnp.where(even, ends[1], ends[0])
    outer[...] = jnp.where(even, ends[0], ends[1])
    for at in range(8):
        spread(at).wait()


def start(even, member, field, dy, weight):
    end = jax.ShapeDtypeStruct((2, 3, 64, 128), bf16)
    return pl.pallas_call(
        start_kernel,
        in_specs=[SMEM, SMEM, ANY, ANY, ANY],
        out_specs=[VMEM, VMEM, ANY],
        out_shape=[end, end, jax.ShapeDtypeStruct((64, 14, 128), bf16)],
        scratch_shapes=[
            pltpu.VMEM((2, 2, 3, 64, 128), bf16),
            pltpu.VMEM((54, 128), f32),
            pltpu.VMEM((8, 14, 128), bf16),
            pltpu.SemaphoreType.DMA((14,)),
        ],
        name="start",
    )(even, member, field, dy, weight)


def z_edges_kernel(field, first, last, tall):
    def one(i, _):
        b, x = lax.div(i, 16), lax.rem(i, 16)
        tall[i] = field[b, x].astype(f32)
        first[b, x] = tall[i, pl.ds(0, 8, stride=8)].astype(bf16)
        last[b, x] = tall[i, pl.ds(7, 8, stride=8)].astype(bf16)
        return 0

    lax.fori_loop(0, 32, one, 0, unroll=4)


def z_edges(field):
    edge = jax.ShapeDtypeStruct((2, 16, 8, 128), bf16)
    return pl.pallas_call(
        z_edges_kernel,
        in_specs=[VMEM],
        out_specs=[VMEM] * 2,
        out_shape=[edge] * 2,
        scratch_shapes=[pltpu.VMEM((32, 64, 128), f32)],
        compiler_params=pltpu.CompilerParams(vmem_limit_bytes=4 * 2**20),
        name="z_edges",
    )(field)


def z_layers(field):
    tall = field.reshape(*field.shape[:2], 8, 8, field.shape[3])
    return tall[:, :, :, 0], tall[:, :, :, 7]


def gate_kernel(value, after, same):
    pass


def gate(value, after):
    space = pl.BlockSpec(memory_space=pl.ANY)
    return pl.pallas_call(
        gate_kernel,
        in_specs=[space, space],
        out_specs=space,
        out_shape=jax.ShapeDtypeStruct(value.shape, value.dtype),
        input_output_aliases={0: 0},
        compiler_params=pltpu.CompilerParams(vmem_limit_bytes=2**20),
        name="gate",
    )(value, after)


def sum_kernel(arrived, after, total):
    total[...] = arrived[...].astype(f32).sum(axis=0)


def sum_of_arrived(arrived, after):
    return pl.pallas_call(
        sum_kernel,
        in_specs=[pl.BlockSpec(memory_space=pltpu.VMEM), pl.BlockSpec(memory_space=pl.ANY)],
        out_shape=jax.ShapeDtypeStruct(arrived.shape[1:], f32),
        compiler_params=pltpu.CompilerParams(vmem_limit_bytes=4 * 2**20),
        cost_estimate=pl.CostEstimate(flops=10**6, bytes_accessed=5 * 10**5, transcendentals=0),
        name="sum_of_arrived",
    )(arrived, after)


def local(acts, weight, moment, second, cotangent):
    crops, _, nx, ny, nz, channels = acts.shape
    field = acts.reshape(crops, nx, ny * nz, channels)
    grad_out = cotangent.reshape(field.shape)
    core = lax.axis_index("sample") % 2
    even = coords()[0] % 2 == 0
    groups = lax.axis_size("space") // (GY * GZ)
    which = jnp.full((1,), core, jnp.int32)
    member = jnp.full((1,), lax.axis_index("sample"), jnp.int32)
    inner, outer, copies = start(jnp.full((1,), even, jnp.int32), member, field, grad_out, weight)
    mine = lax.all_to_all(copies, "space", split_axis=0, concat_axis=0, tiled=True)
    below, above = swapped(inner, outer, even, GY * GZ, groups)

    def along(layers, own):
        pairs = zip(layers(below[:, :2]), own(field), layers(above[:, :2]))
        return [jnp.concatenate(three, 1) for three in pairs]

    zlo, zhi = z_halo(*along(z_layers, z_edges))
    ylo, yhi = y_halo(
        *(
            jnp.concatenate([face, zlo[:, :, at : at + 1], zhi[:, :, at : at + 1]], 2)
            for at, face in zip((0, 7), along(y_layers, y_layers))
        )
    )
    total = crops * lax.axis_size("sample") * lax.axis_size("space") * nx * ny * nz
    beside = chip_swap(mine)
    quarters = (mine, beside, core_swap(mine), core_swap(beside))
    dy = jnp.concatenate([below[:, 2:], grad_out, above[:, 2:]], 1)
    other = core_swap(mine)
    output, dz, windows, kernel = forward(
        member, field, zlo, zhi, ylo, yhi, dy, below, above, quarters
    )
    stays, leaves = weight_grad_halves(which, windows, dz, float(total) ** (-0.5))
    chip = chip_sum(stays, core_swap(leaves))
    ylo, yhi = y_halo(*y_layers(dz), chip)
    zlo, zhi = z_halo(
        *(
            jnp.concatenate([ylo[:, :, at : at + 1], face, yhi[:, :, at : at + 1]], 2)
            for at, face in zip((0, 7), z_layers(dz))
        )
    )
    arrived = lax.all_to_all(chip, "space", split_axis=0, concat_axis=0, tiled=True)
    input_grad, token = backward(dz, ylo, yhi, zlo, zhi, kernel)
    owned = sum_of_arrived(arrived, token)
    owned, across, aslant = (
        [owned + chip_swap(owned), core_swap(owned), diagonal_swap(owned)]
    )
    weight_grad = halves_joined(owned, across + aslant, core, 0)
    new_moment = 0.9 * moment + 0.1 * weight_grad
    new_second = 0.999 * second + 0.001 * weight_grad * weight_grad
    first_fix = 1.0 - 0.9**10
    second_fix = 1.0 - 0.999**10
    new_weight = weight - 0.001 * (new_moment / first_fix) / (
        jnp.sqrt(new_second / second_fix) + 1e-08
    )
    return (
        output.reshape(acts.shape),
        input_grad.reshape(acts.shape),
        weight_grad,
        new_weight,
        new_moment,
        new_second,
    )


def solution(mesh):
    in_specs = (
        P("sample", "space", None, None, None, None),
        P("space", None),
        P("space", None),
        P("space", None),
        P("sample", "space", None, None, None, None),
    )
    out_specs = (
        P("sample", "space", None, None, None, None),
        P("sample", "space", None, None, None, None),
        P("space", None),
        P("space", None),
        P("space", None),
        P("space", None),
    )
    return jax.shard_map(local, mesh=mesh, in_specs=in_specs, out_specs=out_specs, check_vma=False)
```

```python
import functools

import jax
import jax.numpy as jnp
from jax import lax
from jax.experimental import pallas as pl
from jax.experimental.pallas import tpu as pltpu
from jax.sharding import PartitionSpec as P

GY = 2
GZ = 4
FWD_VMEM = 20
QUARTERS = (0, 27, 13, 40)

root_coef = 0.7978845608
cubic_coef = 0.044715
bf16, f32 = jnp.bfloat16, jnp.float32


def activate(pre):
    square = pre * pre
    inner = root_coef * (pre + cubic_coef * pre * square)
    tval = jnp.tanh(inner)
    value = 0.5 * pre * (1.0 + tval)
    slope = 0.5 * (1.0 + tval) + 0.5 * pre * (1.0 - tval * tval) * root_coef * (
        1.0 + 3.0 * cubic_coef * square
    )
    return (value, slope)


def fill_windows(windows, start, layers, source):
    place = lax.broadcasted_iota(jnp.int32, (8, 128), 0)

    def one(x, _):
        at = start + x
        shifted = [[], [], []]
        for row, low, high in source(x):
            lo, hi = jnp.broadcast_to(low, (8, 128)), jnp.broadcast_to(high, (8, 128))
            shifted[0].append(jnp.where(place == 0, lo, pltpu.roll(row, 1, 0)))
            shifted[1].append(row)
            shifted[2].append(jnp.where(place == 7, hi, pltpu.roll(row, 7, 0)))
        for ky in range(3):
            for kz in range(3):
                col = (ky * 3 + kz) * 128
                tile = jnp.concatenate(shifted[kz][ky : ky + 8], axis=0).astype(bf16)
                windows[lax.div(at, 2), lax.rem(at, 2), :, col : col + 128] = tile
        return 0

    lax.fori_loop(0, layers, one, 0)


def z_first_source(b, center, zlo, zhi, ylo, yhi, ahead=0):
    def source(x):
        at = x + ahead
        wide, low, high = (ref.astype(f32) for ref in (center[b, x], zlo[b, at], zhi[b, at]))
        below, above = ylo[b, at].astype(f32), yhi[b, at].astype(f32)
        rows = [(below[0:8], below[8:9], below[9:10])]
        rows += [(wide[8 * y : 8 * y + 8], low[y : y + 1], high[y : y + 1]) for y in range(8)]
        return rows + [(above[0:8], above[8:9], above[9:10])]

    return source


def y_first_source(b, center, ylo, yhi, zlo, zhi):
    def source(x):
        wide, low, high = (ref.astype(f32) for ref in (center[b, x], zlo[b, x], zhi[b, x]))
        rows = [ylo[b, x].astype(f32)] + [wide[8 * y : 8 * y + 8] for y in range(8)]
        rows += [yhi[b, x].astype(f32)]
        return [(rows[y], low[y : y + 1], high[y : y + 1]) for y in range(10)]

    return source


def pair_kernels(kern, wide):
    none = jnp.zeros((1152, 128), bf16)
    for at in range(4):
        wide[at, :, 0:128] = kern[at] if at < 3 else none
        wide[at, :, 128:256] = kern[at - 1] if at > 0 else none


def pair_products(windows, wide, pairs):
    total = jnp.zeros((64 * pairs, 256), f32)
    for at in range(4):
        lhs = windows[at // 2 : at // 2 + pairs, at % 2].reshape(64 * pairs, 1152)
        total += jnp.dot(lhs, wide[at], preferred_element_type=f32)
    return total


def forward_kernel(member_ref, center, zlo, zhi, ylo, yhi, dy, below, above, own, chip, core, slant,
                   out, dz, windows, kern, rows, wide):
    member = member_ref[0]
    side, half = lax.div(member, 2), lax.rem(member, 2)
    near, far = 27 * half, 27 - 27 * half
    starts = (near + 13 * side, near + 13 - 13 * side, far + 13 * side, far + 13 - 13 * side)

    def piece(s, _):
        for quarter, first in zip((own, chip, core, slant), starts):
            rows[pl.ds(54 * s + first, 14), :] = quarter[s].astype(f32)
        return 0

    lax.fori_loop(0, 64, piece, 0)
    for kx in range(3):
        kern[kx] = rows[1152 * kx : 1152 * (kx + 1), :].astype(bf16)
    pair_kernels(kern, wide)
    halo = (zlo, zhi, ylo, yhi)

    def crop(b, _):
        here = windows.at[b]
        fill_windows(here, 0, 2, z_first_source(b, below, *halo))
        fill_windows(here, 2, 16, z_first_source(b, center, *halo, 2))
        fill_windows(here, 18, 2, z_first_source(b, above, *halo, 18))
        both = pair_products(here, wide, 9)
        for at in range(2):
            value, slope = activate(both[:, 128 * at : 128 * (at + 1)])
            grad = dy[b, :, at].reshape(576, 128).astype(f32) * slope
            dz[b, :, at] = grad.astype(bf16).reshape(9, 64, 128)
            value = value.astype(bf16).reshape(9, 64, 128)
            out[b, :, 1 - at] = value[1:9] if at == 0 else value[0:8]
        return 0

    lax.fori_loop(0, 2, crop, 0)


VMEM = pl.BlockSpec(memory_space=pltpu.VMEM)
SMEM = pl.BlockSpec(memory_space=pltpu.SMEM)
ANY = pl.BlockSpec(memory_space=pl.ANY)


def forward(member, center, zlo, zhi, ylo, yhi, dy, below, above, quarters):
    ins = (center, zlo, zhi, ylo, yhi, dy.reshape(2, 9, 2, 64, 128), below, above, *quarters)
    outs = [
        jax.ShapeDtypeStruct((2, 8, 2, 64, 128), bf16),
        jax.ShapeDtypeStruct((2, 9, 2, 64, 128), bf16),
        jax.ShapeDtypeStruct((2, 10, 2, 64, 1152), bf16),
        jax.ShapeDtypeStruct((3, 1152, 128), bf16),
    ]
    out, dz, windows, kern = pl.pallas_call(
        forward_kernel,
        in_specs=[SMEM] + [VMEM] * len(ins),
        out_specs=[VMEM] * 4,
        out_shape=outs,
        scratch_shapes=[pltpu.VMEM((3488, 128), f32), pltpu.VMEM((4, 1152, 256), bf16)],
        compiler_params=pltpu.CompilerParams(vmem_limit_bytes=FWD_VMEM * 2**20),
        cost_estimate=pl.CostEstimate(flops=4 * 10**9, bytes_accessed=8 * 10**6, transcendentals=300000),
        name="forward",
    )(member, *ins)
    return out, dz.reshape(2, 18, 64, 128), windows.reshape(2, 20, 64, 1152), kern


def weight_grad_kernel(scale, core_ref, windows, dz, stays, leaves, rows, dzs, total):
    core = core_ref[0]
    dzs[...] = jnp.zeros_like(dzs)
    for b in range(2):
        own = dz[b, 1:17].reshape(1024, 128)
        for kx in range(3):
            dzs[64 * kx : 64 * kx + 1024, 128 * kx : 128 * (kx + 1)] = own
        both = windows[b, 1:19].reshape(1152, 1152)
        term = lax.dot_general(dzs[...], both, (((0,), (0,)), ((), ())), preferred_element_type=f32)
        if b == 0:
            total[...] = term
    whole = (total[...] + term) * scale
    for kx in range(3):
        for t in range(9):
            block = whole[128 * kx : 128 * (kx + 1), 128 * t : 128 * (t + 1)]
            row = (kx * 9 + t) * 128
            rows[row : row + 128, :] = block.T

    def piece(s, _):
        low, high = rows[pl.ds(54 * s, 27), :], rows[pl.ds(54 * s + 27, 27), :]
        stays[s] = jnp.where(core == 0, low, high).astype(bf16)
        leaves[s] = jnp.where(core == 0, high, low).astype(bf16)
        return 0

    lax.fori_loop(0, 64, piece, 0)


def weight_grad_halves(core, windows, dz, scale):
    half = jax.ShapeDtypeStruct((64, 27, 128), bf16)
    return pl.pallas_call(
        functools.partial(weight_grad_kernel, scale),
        in_specs=[SMEM, VMEM, VMEM],
        out_specs=[VMEM] * 2,
        out_shape=[half] * 2,
        scratch_shapes=[
            pltpu.VMEM((3488, 128), f32),
            pltpu.VMEM((1152, 384), bf16),
            pltpu.VMEM((384, 1152), f32),
        ],
        compiler_params=pltpu.CompilerParams(vmem_limit_bytes=FWD_VMEM * 2**20),
        cost_estimate=pl.CostEstimate(flops=4 * 10**9, bytes_accessed=7 * 10**6, transcendentals=0),
        name="weight_grad_halves",
    )(core, windows, dz)


def chip_kernel(stays, got, chip):
    chip[...] = (stays[...].astype(f32) + got[...].astype(f32)).astype(bf16)


def chip_sum(stays, got):
    vmem = pl.BlockSpec(memory_space=pltpu.VMEM)
    return pl.pallas_call(
        chip_kernel,
        in_specs=[vmem, vmem],
        out_specs=vmem,
        out_shape=jax.ShapeDtypeStruct(stays.shape, bf16),
        compiler_params=pltpu.CompilerParams(vmem_limit_bytes=4 * 2**20),
        name="chip_sum",
    )(stays, got)


def flipped_pair_kernels(kern, wide):
    none = jnp.zeros((128, 1152), bf16)
    for at in range(4):
        for side, kx in ((0, 2 - at), (1, 3 - at)):
            if not 0 <= kx <= 2:
                wide[at, 128 * side : 128 * (side + 1), :] = none
                continue
            for tap in range(9):
                col = 128 * (8 - tap)
                block = kern[kx, 128 * tap : 128 * (tap + 1), :]
                wide[at, 128 * side : 128 * (side + 1), col : col + 128] = block


def backward_kernel(center, ylo, yhi, zlo, zhi, kern, out, token, windows, wide):
    token[...] = jnp.zeros_like(token)
    flipped_pair_kernels(kern, wide)

    def crop(b, _):
        fill_windows(windows, 0, 18, y_first_source(b, center, ylo, yhi, zlo, zhi))
        both = jnp.zeros((512, 256), f32)
        for at in range(4):
            lhs = windows[at // 2 : at // 2 + 8, at % 2].reshape(512, 1152)
            both += lax.dot_general(lhs, wide[at], (((1,), (1,)), ((), ())), preferred_element_type=f32)
        for side in range(2):
            grad = both[:, 128 * side : 128 * (side + 1)].astype(bf16)
            out[b, :, side] = grad.reshape(8, 64, 128)
        return 0

    lax.fori_loop(0, 2, crop, 0)


def backward(center, ylo, yhi, zlo, zhi, kern):
    return pl.pallas_call(
        backward_kernel,
        in_specs=[VMEM] * 6,
        out_specs=[VMEM] * 2,
        out_shape=[jax.ShapeDtypeStruct((2, 8, 2, 64, 128), bf16), jax.ShapeDtypeStruct((8, 128), f32)],
        scratch_shapes=[pltpu.VMEM((9, 2, 64, 1152), bf16), pltpu.VMEM((4, 256, 1152), bf16)],
        compiler_params=pltpu.CompilerParams(vmem_limit_bytes=FWD_VMEM * 2**20),
        cost_estimate=pl.CostEstimate(flops=4 * 10**9, bytes_accessed=3 * 10**6, transcendentals=0),
        name="backward",
    )(center, ylo, yhi, zlo, zhi, kern)


def flip_pairs(count, bit):
    return [(i, i ^ bit) for i in range(count)]


def odd_pairs(count, stride, length):
    pairs = []
    for i in range(count):
        coord = i // stride % length
        other = coord + 1 if coord % 2 == 1 else coord - 1
        if 0 <= other < length:
            pairs.append((i, i + (other - coord) * stride))
    return pairs


def swapped(inner, outer, even, stride, length):
    devices = lax.axis_size("space")
    inner = lax.ppermute(inner, "space", flip_pairs(devices, stride))
    outer = lax.ppermute(outer, "space", odd_pairs(devices, stride, length))
    return jnp.where(even, outer, inner), jnp.where(even, inner, outer)


def swap_layers(first, last, coord, stride, length):
    even = coord % 2 == 0
    return swapped(jnp.where(even, last, first), jnp.where(even, first, last), even, stride, length)


def core_swap(value):
    return lax.ppermute(value, "sample", flip_pairs(lax.axis_size("sample"), 1))


def chip_swap(value):
    return lax.ppermute(value, "sample", flip_pairs(lax.axis_size("sample"), 2))


def diagonal_swap(value):
    return lax.ppermute(value, "sample", flip_pairs(lax.axis_size("sample"), 3))


def halves_joined(mine, other, core, dim):
    low = jnp.where(core == 0, mine, other)
    high = jnp.where(core == 0, other, mine)
    return jnp.concatenate([low, high], dim)


def coords():
    place = lax.axis_index("space")
    return place // (GZ * GY), place // GZ % GY, place % GZ


def y_halo(first, last, after=None):
    coord_y = coords()[1]
    face = jnp.where(coord_y == 0, last, first)
    got = lax.ppermute(face, "space", flip_pairs(lax.axis_size("space"), GZ))
    got = got if after is None else gate(got, after)
    none = jnp.zeros_like(got)
    return jnp.where(coord_y == 0, none, got), jnp.where(coord_y == 0, got, none)


def y_layers(field):
    return field[:, :, :8], field[:, :, -8:]


def z_halo(first, last):
    return swap_layers(first, last, coords()[2], 1, GZ)


def start_kernel(even_ref, member_ref, field, dy, weight, inner, outer, copies, ends, rows, wide, sems):
    def spread(at):
        return pltpu.make_async_copy(wide, copies.at[pl.ds(8 * at, 8)], sems.at[6 + at])

    fetches = [pltpu.make_async_copy(weight, rows, sems.at[0])]
    for at, x in ((0, 0), (1, 14)):
        fetches.append(pltpu.make_async_copy(field.at[:, x : x + 2], ends.at[at, :, 0:2], sems.at[1 + 2 * at]))
        x = 15 * at
        fetches.append(pltpu.make_async_copy(dy.at[:, x : x + 1], ends.at[at, :, 2:3], sems.at[2 + 2 * at]))
    for fetch in fetches:
        fetch.start()
    even, member = even_ref[0] == 1, member_ref[0]
    fetches[0].wait()
    share = rows[0:14]
    for at in range(1, 4):
        share = jnp.where(member == at, rows[QUARTERS[at] : QUARTERS[at] + 14], share)
    for at in range(8):
        wide[at] = share.astype(bf16)
    for at in range(8):
        spread(at).start()
    for fetch in fetches[1:]:
        fetch.wait()
    inner[...] = jnp.where(even, ends[1], ends[0])
    outer[...] = jnp.where(even, ends[0], ends[1])
    for at in range(8):
        spread(at).wait()


def start(even, member, field, dy, weight):
    end = jax.ShapeDtypeStruct((2, 3, 64, 128), bf16)
    return pl.pallas_call(
        start_kernel,
        in_specs=[SMEM, SMEM, ANY, ANY, ANY],
        out_specs=[VMEM, VMEM, ANY],
        out_shape=[end, end, jax.ShapeDtypeStruct((64, 14, 128), bf16)],
        scratch_shapes=[
            pltpu.VMEM((2, 2, 3, 64, 128), bf16),
            pltpu.VMEM((54, 128), f32),
            pltpu.VMEM((8, 14, 128), bf16),
            pltpu.SemaphoreType.DMA((14,)),
        ],
        name="start",
    )(even, member, field, dy, weight)


def edges_kernel(field, yfirst, ylast, zfirst, zlast, tall):
    def one(i, _):
        b, x = lax.div(i, 16), lax.rem(i, 16)
        wide = field[b, x].astype(f32)
        tall[i] = wide
        yfirst[b, x] = wide[0:8].astype(bf16)
        ylast[b, x] = wide[56:64].astype(bf16)
        zfirst[b, x] = tall[i, pl.ds(0, 8, stride=8)].astype(bf16)
        zlast[b, x] = tall[i, pl.ds(7, 8, stride=8)].astype(bf16)
        return 0

    lax.fori_loop(0, 32, one, 0, unroll=4)


def edges(field):
    edge = jax.ShapeDtypeStruct((2, 16, 8, 128), bf16)
    return pl.pallas_call(
        edges_kernel,
        in_specs=[VMEM],
        out_specs=[VMEM] * 4,
        out_shape=[edge] * 4,
        scratch_shapes=[pltpu.VMEM((32, 64, 128), f32)],
        compiler_params=pltpu.CompilerParams(vmem_limit_bytes=4 * 2**20),
        name="edges",
    )(field)


def z_layers(field):
    tall = field.reshape(*field.shape[:2], 8, 8, field.shape[3])
    return tall[:, :, :, 0], tall[:, :, :, 7]


def gate_kernel(value, after, same):
    pass


def gate(value, after):
    space = pl.BlockSpec(memory_space=pl.ANY)
    return pl.pallas_call(
        gate_kernel,
        in_specs=[space, space],
        out_specs=space,
        out_shape=jax.ShapeDtypeStruct(value.shape, value.dtype),
        input_output_aliases={0: 0},
        compiler_params=pltpu.CompilerParams(vmem_limit_bytes=2**20),
        name="gate",
    )(value, after)


def sum_kernel(arrived, after, total):
    total[...] = arrived[...].astype(f32).sum(axis=0)


def sum_of_arrived(arrived, after):
    return pl.pallas_call(
        sum_kernel,
        in_specs=[pl.BlockSpec(memory_space=pltpu.VMEM), pl.BlockSpec(memory_space=pl.ANY)],
        out_shape=jax.ShapeDtypeStruct(arrived.shape[1:], f32),
        compiler_params=pltpu.CompilerParams(vmem_limit_bytes=4 * 2**20),
        cost_estimate=pl.CostEstimate(flops=10**6, bytes_accessed=5 * 10**5, transcendentals=0),
        name="sum_of_arrived",
    )(arrived, after)


def local(acts, weight, moment, second, cotangent):
    crops, _, nx, ny, nz, channels = acts.shape
    field = acts.reshape(crops, nx, ny * nz, channels)
    grad_out = cotangent.reshape(field.shape)
    core = lax.axis_index("sample") % 2
    even = coords()[0] % 2 == 0
    groups = lax.axis_size("space") // (GY * GZ)
    which = jnp.full((1,), core, jnp.int32)
    member = jnp.full((1,), lax.axis_index("sample"), jnp.int32)
    inner, outer, copies = start(jnp.full((1,), even, jnp.int32), member, field, grad_out, weight)
    mine = lax.all_to_all(copies, "space", split_axis=0, concat_axis=0, tiled=True)
    below, above = swapped(inner, outer, even, GY * GZ, groups)

    faces = edges(field)

    def along(layers, own):
        pairs = zip(layers(below[:, :2]), own, layers(above[:, :2]))
        return [jnp.concatenate(three, 1) for three in pairs]

    zlo, zhi = z_halo(*along(z_layers, faces[2:]))
    ylo, yhi = y_halo(
        *(
            jnp.concatenate([face, zlo[:, :, at : at + 1], zhi[:, :, at : at + 1]], 2)
            for at, face in zip((0, 7), along(y_layers, faces[:2]))
        )
    )
    total = crops * lax.axis_size("sample") * lax.axis_size("space") * nx * ny * nz
    beside = chip_swap(mine)
    quarters = (mine, beside, core_swap(mine), core_swap(beside))
    dy = jnp.concatenate([below[:, 2:], grad_out, above[:, 2:]], 1)
    other = core_swap(mine)
    output, dz, windows, kernel = forward(
        member, field, zlo, zhi, ylo, yhi, dy, below, above, quarters
    )
    stays, leaves = weight_grad_halves(which, windows, dz, float(total) ** (-0.5))
    chip = chip_sum(stays, core_swap(leaves))
    ylo, yhi = y_halo(*y_layers(dz), chip)
    zlo, zhi = z_halo(
        *(
            jnp.concatenate([ylo[:, :, at : at + 1], face, yhi[:, :, at : at + 1]], 2)
            for at, face in zip((0, 7), z_layers(dz))
        )
    )
    arrived = lax.all_to_all(chip, "space", split_axis=0, concat_axis=0, tiled=True)
    input_grad, token = backward(dz, ylo, yhi, zlo, zhi, kernel)
    owned = sum_of_arrived(arrived, token)
    owned, across, aslant = (
        [owned + chip_swap(owned), core_swap(owned), diagonal_swap(owned)]
    )
    weight_grad = halves_joined(owned, across + aslant, core, 0)
    new_moment = 0.9 * moment + 0.1 * weight_grad
    new_second = 0.999 * second + 0.001 * weight_grad * weight_grad
    first_fix = 1.0 - 0.9**10
    second_fix = 1.0 - 0.999**10
    new_weight = weight - 0.001 * (new_moment / first_fix) / (
        jnp.sqrt(new_second / second_fix) + 1e-08
    )
    return (
        output.reshape(acts.shape),
        input_grad.reshape(acts.shape),
        weight_grad,
        new_weight,
        new_moment,
        new_second,
    )


def solution(mesh):
    in_specs = (
        P("sample", "space", None, None, None, None),
        P("space", None),
        P("space", None),
        P("space", None),
        P("sample", "space", None, None, None, None),
    )
    out_specs = (
        P("sample", "space", None, None, None, None),
        P("sample", "space", None, None, None, None),
        P("space", None),
        P("space", None),
        P("space", None),
        P("space", None),
    )
    return jax.shard_map(local, mesh=mesh, in_specs=in_specs, out_specs=out_specs, check_vma=False)
```

```python
import functools

import jax
import jax.numpy as jnp
from jax import lax
from jax.experimental import pallas as pl
from jax.experimental.pallas import tpu as pltpu
from jax.sharding import PartitionSpec as P

GY = 2
GZ = 4
FWD_VMEM = 20
QUARTERS = (0, 27, 13, 40)

root_coef = 0.7978845608
cubic_coef = 0.044715
bf16, f32 = jnp.bfloat16, jnp.float32


def activate(pre):
    square = pre * pre
    inner = root_coef * (pre + cubic_coef * pre * square)
    tval = jnp.tanh(inner)
    value = 0.5 * pre * (1.0 + tval)
    slope = 0.5 * (1.0 + tval) + 0.5 * pre * (1.0 - tval * tval) * root_coef * (
        1.0 + 3.0 * cubic_coef * square
    )
    return (value, slope)


def fill_windows(windows, start, layers, source):
    place = lax.broadcasted_iota(jnp.int32, (8, 128), 0)

    def one(x, _):
        at = start + x
        shifted = [[], [], []]
        for row, low, high in source(x):
            lo, hi = jnp.broadcast_to(low, (8, 128)), jnp.broadcast_to(high, (8, 128))
            shifted[0].append(jnp.where(place == 0, lo, pltpu.roll(row, 1, 0)))
            shifted[1].append(row)
            shifted[2].append(jnp.where(place == 7, hi, pltpu.roll(row, 7, 0)))
        for ky in range(3):
            for kz in range(3):
                col = (ky * 3 + kz) * 128
                tile = jnp.concatenate(shifted[kz][ky : ky + 8], axis=0).astype(bf16)
                windows[lax.div(at, 2), lax.rem(at, 2), :, col : col + 128] = tile
        return 0

    lax.fori_loop(0, layers, one, 0, unroll=2)


def z_first_source(b, center, zlo, zhi, ylo, yhi, ahead=0):
    def source(x):
        at = x + ahead
        wide, low, high = (ref.astype(f32) for ref in (center[b, x], zlo[b, at], zhi[b, at]))
        below, above = ylo[b, at].astype(f32), yhi[b, at].astype(f32)
        rows = [(below[0:8], below[8:9], below[9:10])]
        rows += [(wide[8 * y : 8 * y + 8], low[y : y + 1], high[y : y + 1]) for y in range(8)]
        return rows + [(above[0:8], above[8:9], above[9:10])]

    return source


def y_first_source(b, center, ylo, yhi, zlo, zhi):
    def source(x):
        wide, low, high = (ref.astype(f32) for ref in (center[b, x], zlo[b, x], zhi[b, x]))
        rows = [ylo[b, x].astype(f32)] + [wide[8 * y : 8 * y + 8] for y in range(8)]
        rows += [yhi[b, x].astype(f32)]
        return [(rows[y], low[y : y + 1], high[y : y + 1]) for y in range(10)]

    return source


def pair_kernels(kern, wide):
    none = jnp.zeros((1152, 128), bf16)
    for at in range(4):
        wide[at, :, 0:128] = kern[at] if at < 3 else none
        wide[at, :, 128:256] = kern[at - 1] if at > 0 else none


def pair_products(windows, wide, pairs):
    total = jnp.zeros((64 * pairs, 256), f32)
    for at in range(4):
        lhs = windows[at // 2 : at // 2 + pairs, at % 2].reshape(64 * pairs, 1152)
        total += jnp.dot(lhs, wide[at], preferred_element_type=f32)
    return total


def forward_kernel(member_ref, center, zlo, zhi, ylo, yhi, dy, below, above, own, chip, core, slant,
                   out, dz, windows, kern, rows, wide):
    member = member_ref[0]
    side, half = lax.div(member, 2), lax.rem(member, 2)
    near, far = 27 * half, 27 - 27 * half
    starts = (near + 13 * side, near + 13 - 13 * side, far + 13 * side, far + 13 - 13 * side)

    def piece(s, _):
        for quarter, first in zip((own, chip, core, slant), starts):
            rows[pl.ds(54 * s + first, 14), :] = quarter[s].astype(f32)
        return 0

    lax.fori_loop(0, 64, piece, 0, unroll=4)
    for kx in range(3):
        kern[kx] = rows[1152 * kx : 1152 * (kx + 1), :].astype(bf16)
    pair_kernels(kern, wide)
    halo = (zlo, zhi, ylo, yhi)

    def crop(b, _):
        here = windows.at[b]
        fill_windows(here, 0, 2, z_first_source(b, below, *halo))
        fill_windows(here, 2, 16, z_first_source(b, center, *halo, 2))
        fill_windows(here, 18, 2, z_first_source(b, above, *halo, 18))
        both = pair_products(here, wide, 9)
        for at in range(2):
            value, slope = activate(both[:, 128 * at : 128 * (at + 1)])
            grad = dy[b, :, at].reshape(576, 128).astype(f32) * slope
            dz[b, :, at] = grad.astype(bf16).reshape(9, 64, 128)
            value = value.astype(bf16).reshape(9, 64, 128)
            out[b, :, 1 - at] = value[1:9] if at == 0 else value[0:8]
        return 0

    lax.fori_loop(0, 2, crop, 0)


VMEM = pl.BlockSpec(memory_space=pltpu.VMEM)
SMEM = pl.BlockSpec(memory_space=pltpu.SMEM)
ANY = pl.BlockSpec(memory_space=pl.ANY)


def forward(member, center, zlo, zhi, ylo, yhi, dy, below, above, quarters):
    ins = (center, zlo, zhi, ylo, yhi, dy.reshape(2, 9, 2, 64, 128), below, above, *quarters)
    outs = [
        jax.ShapeDtypeStruct((2, 8, 2, 64, 128), bf16),
        jax.ShapeDtypeStruct((2, 9, 2, 64, 128), bf16),
        jax.ShapeDtypeStruct((2, 10, 2, 64, 1152), bf16),
        jax.ShapeDtypeStruct((3, 1152, 128), bf16),
    ]
    out, dz, windows, kern = pl.pallas_call(
        forward_kernel,
        in_specs=[SMEM] + [VMEM] * len(ins),
        out_specs=[VMEM] * 4,
        out_shape=outs,
        scratch_shapes=[pltpu.VMEM((3488, 128), f32), pltpu.VMEM((4, 1152, 256), bf16)],
        compiler_params=pltpu.CompilerParams(vmem_limit_bytes=FWD_VMEM * 2**20),
        cost_estimate=pl.CostEstimate(flops=4 * 10**9, bytes_accessed=8 * 10**6, transcendentals=300000),
        name="forward",
    )(member, *ins)
    return out, dz.reshape(2, 18, 64, 128), windows.reshape(2, 20, 64, 1152), kern


def weight_grad_kernel(scale, core_ref, windows, dz, stays, leaves, rows, dzs, total):
    core = core_ref[0]
    dzs[...] = jnp.zeros_like(dzs)
    for b in range(2):
        own = dz[b, 1:17].reshape(1024, 128)
        for kx in range(3):
            dzs[64 * kx : 64 * kx + 1024, 128 * kx : 128 * (kx + 1)] = own
        both = windows[b, 1:19].reshape(1152, 1152)
        term = lax.dot_general(dzs[...], both, (((0,), (0,)), ((), ())), preferred_element_type=f32)
        if b == 0:
            total[...] = term
    whole = (total[...] + term) * scale
    for kx in range(3):
        for t in range(9):
            block = whole[128 * kx : 128 * (kx + 1), 128 * t : 128 * (t + 1)]
            row = (kx * 9 + t) * 128
            rows[row : row + 128, :] = block.T

    def piece(s, _):
        low, high = rows[pl.ds(54 * s, 27), :], rows[pl.ds(54 * s + 27, 27), :]
        stays[s] = jnp.where(core == 0, low, high).astype(bf16)
        leaves[s] = jnp.where(core == 0, high, low).astype(bf16)
        return 0

    lax.fori_loop(0, 64, piece, 0, unroll=4)


def weight_grad_halves(core, windows, dz, scale):
    half = jax.ShapeDtypeStruct((64, 27, 128), bf16)
    return pl.pallas_call(
        functools.partial(weight_grad_kernel, scale),
        in_specs=[SMEM, VMEM, VMEM],
        out_specs=[VMEM] * 2,
        out_shape=[half] * 2,
        scratch_shapes=[
            pltpu.VMEM((3488, 128), f32),
            pltpu.VMEM((1152, 384), bf16),
            pltpu.VMEM((384, 1152), f32),
        ],
        compiler_params=pltpu.CompilerParams(vmem_limit_bytes=FWD_VMEM * 2**20),
        cost_estimate=pl.CostEstimate(flops=4 * 10**9, bytes_accessed=7 * 10**6, transcendentals=0),
        name="weight_grad_halves",
    )(core, windows, dz)


def chip_kernel(stays, got, chip):
    chip[...] = (stays[...].astype(f32) + got[...].astype(f32)).astype(bf16)


def chip_sum(stays, got):
    vmem = pl.BlockSpec(memory_space=pltpu.VMEM)
    return pl.pallas_call(
        chip_kernel,
        in_specs=[vmem, vmem],
        out_specs=vmem,
        out_shape=jax.ShapeDtypeStruct(stays.shape, bf16),
        compiler_params=pltpu.CompilerParams(vmem_limit_bytes=4 * 2**20),
        name="chip_sum",
    )(stays, got)


def flipped_pair_kernels(kern, wide):
    none = jnp.zeros((128, 1152), bf16)
    for at in range(4):
        for side, kx in ((0, 2 - at), (1, 3 - at)):
            if not 0 <= kx <= 2:
                wide[at, 128 * side : 128 * (side + 1), :] = none
                continue
            for tap in range(9):
                col = 128 * (8 - tap)
                block = kern[kx, 128 * tap : 128 * (tap + 1), :]
                wide[at, 128 * side : 128 * (side + 1), col : col + 128] = block


def backward_kernel(center, ylo, yhi, zlo, zhi, kern, out, token, windows, wide):
    token[...] = jnp.zeros_like(token)
    flipped_pair_kernels(kern, wide)

    def crop(b, _):
        fill_windows(windows, 0, 18, y_first_source(b, center, ylo, yhi, zlo, zhi))
        both = jnp.zeros((512, 256), f32)
        for at in range(4):
            lhs = windows[at // 2 : at // 2 + 8, at % 2].reshape(512, 1152)
            both += lax.dot_general(lhs, wide[at], (((1,), (1,)), ((), ())), preferred_element_type=f32)
        for side in range(2):
            grad = both[:, 128 * side : 128 * (side + 1)].astype(bf16)
            out[b, :, side] = grad.reshape(8, 64, 128)
        return 0

    lax.fori_loop(0, 2, crop, 0)


def backward(center, ylo, yhi, zlo, zhi, kern):
    return pl.pallas_call(
        backward_kernel,
        in_specs=[VMEM] * 6,
        out_specs=[VMEM] * 2,
        out_shape=[jax.ShapeDtypeStruct((2, 8, 2, 64, 128), bf16), jax.ShapeDtypeStruct((8, 128), f32)],
        scratch_shapes=[pltpu.VMEM((9, 2, 64, 1152), bf16), pltpu.VMEM((4, 256, 1152), bf16)],
        compiler_params=pltpu.CompilerParams(vmem_limit_bytes=FWD_VMEM * 2**20),
        cost_estimate=pl.CostEstimate(flops=4 * 10**9, bytes_accessed=3 * 10**6, transcendentals=0),
        name="backward",
    )(center, ylo, yhi, zlo, zhi, kern)


def flip_pairs(count, bit):
    return [(i, i ^ bit) for i in range(count)]


def odd_pairs(count, stride, length):
    pairs = []
    for i in range(count):
        coord = i // stride % length
        other = coord + 1 if coord % 2 == 1 else coord - 1
        if 0 <= other < length:
            pairs.append((i, i + (other - coord) * stride))
    return pairs


def swapped(inner, outer, even, stride, length):
    devices = lax.axis_size("space")
    inner = lax.ppermute(inner, "space", flip_pairs(devices, stride))
    outer = lax.ppermute(outer, "space", odd_pairs(devices, stride, length))
    return jnp.where(even, outer, inner), jnp.where(even, inner, outer)


def swap_layers(first, last, coord, stride, length):
    even = coord % 2 == 0
    return swapped(jnp.where(even, last, first), jnp.where(even, first, last), even, stride, length)


def core_swap(value):
    return lax.ppermute(value, "sample", flip_pairs(lax.axis_size("sample"), 1))


def chip_swap(value):
    return lax.ppermute(value, "sample", flip_pairs(lax.axis_size("sample"), 2))


def diagonal_swap(value):
    return lax.ppermute(value, "sample", flip_pairs(lax.axis_size("sample"), 3))


def halves_joined(mine, other, core, dim):
    low = jnp.where(core == 0, mine, other)
    high = jnp.where(core == 0, other, mine)
    return jnp.concatenate([low, high], dim)


def coords():
    place = lax.axis_index("space")
    return place // (GZ * GY), place // GZ % GY, place % GZ


def y_halo(first, last, after=None):
    coord_y = coords()[1]
    face = jnp.where(coord_y == 0, last, first)
    got = lax.ppermute(face, "space", flip_pairs(lax.axis_size("space"), GZ))
    got = got if after is None else gate(got, after)
    none = jnp.zeros_like(got)
    return jnp.where(coord_y == 0, none, got), jnp.where(coord_y == 0, got, none)


def y_layers(field):
    return field[:, :, :8], field[:, :, -8:]


def z_halo(first, last):
    return swap_layers(first, last, coords()[2], 1, GZ)


def start_kernel(even_ref, member_ref, field, dy, weight, inner, outer, copies, ends, rows, wide, sems):
    def spread(at):
        return pltpu.make_async_copy(wide, copies.at[pl.ds(8 * at, 8)], sems.at[6 + at])

    fetches = [pltpu.make_async_copy(weight, rows, sems.at[0])]
    for at, x in ((0, 0), (1, 14)):
        fetches.append(pltpu.make_async_copy(field.at[:, x : x + 2], ends.at[at, :, 0:2], sems.at[1 + 2 * at]))
        x = 15 * at
        fetches.append(pltpu.make_async_copy(dy.at[:, x : x + 1], ends.at[at, :, 2:3], sems.at[2 + 2 * at]))
    for fetch in fetches:
        fetch.start()
    even, member = even_ref[0] == 1, member_ref[0]
    fetches[0].wait()
    share = rows[0:14]
    for at in range(1, 4):
        share = jnp.where(member == at, rows[QUARTERS[at] : QUARTERS[at] + 14], share)
    for at in range(8):
        wide[at] = share.astype(bf16)
    for at in range(8):
        spread(at).start()
    for fetch in fetches[1:]:
        fetch.wait()
    inner[...] = jnp.where(even, ends[1], ends[0])
    outer[...] = jnp.where(even, ends[0], ends[1])
    for at in range(8):
        spread(at).wait()


def start(even, member, field, dy, weight):
    end = jax.ShapeDtypeStruct((2, 3, 64, 128), bf16)
    return pl.pallas_call(
        start_kernel,
        in_specs=[SMEM, SMEM, ANY, ANY, ANY],
        out_specs=[VMEM, VMEM, ANY],
        out_shape=[end, end, jax.ShapeDtypeStruct((64, 14, 128), bf16)],
        scratch_shapes=[
            pltpu.VMEM((2, 2, 3, 64, 128), bf16),
            pltpu.VMEM((54, 128), f32),
            pltpu.VMEM((8, 14, 128), bf16),
            pltpu.SemaphoreType.DMA((14,)),
        ],
        name="start",
    )(even, member, field, dy, weight)


def edges_kernel(field, yfirst, ylast, zfirst, zlast, tall):
    def one(i, _):
        b, x = lax.div(i, 16), lax.rem(i, 16)
        wide = field[b, x].astype(f32)
        tall[i] = wide
        yfirst[b, x] = wide[0:8].astype(bf16)
        ylast[b, x] = wide[56:64].astype(bf16)
        zfirst[b, x] = tall[i, pl.ds(0, 8, stride=8)].astype(bf16)
        zlast[b, x] = tall[i, pl.ds(7, 8, stride=8)].astype(bf16)
        return 0

    lax.fori_loop(0, 32, one, 0, unroll=4)


def edges(field):
    edge = jax.ShapeDtypeStruct((2, 16, 8, 128), bf16)
    return pl.pallas_call(
        edges_kernel,
        in_specs=[VMEM],
        out_specs=[VMEM] * 4,
        out_shape=[edge] * 4,
        scratch_shapes=[pltpu.VMEM((32, 64, 128), f32)],
        compiler_params=pltpu.CompilerParams(vmem_limit_bytes=4 * 2**20),
        name="edges",
    )(field)


def z_layers(field):
    tall = field.reshape(*field.shape[:2], 8, 8, field.shape[3])
    return tall[:, :, :, 0], tall[:, :, :, 7]


def gate_kernel(value, after, same):
    pass


def gate(value, after):
    space = pl.BlockSpec(memory_space=pl.ANY)
    return pl.pallas_call(
        gate_kernel,
        in_specs=[space, space],
        out_specs=space,
        out_shape=jax.ShapeDtypeStruct(value.shape, value.dtype),
        input_output_aliases={0: 0},
        compiler_params=pltpu.CompilerParams(vmem_limit_bytes=2**20),
        name="gate",
    )(value, after)


def sum_kernel(arrived, after, total):
    total[...] = arrived[...].astype(f32).sum(axis=0)


def sum_of_arrived(arrived, after):
    return pl.pallas_call(
        sum_kernel,
        in_specs=[pl.BlockSpec(memory_space=pltpu.VMEM), pl.BlockSpec(memory_space=pl.ANY)],
        out_shape=jax.ShapeDtypeStruct(arrived.shape[1:], f32),
        compiler_params=pltpu.CompilerParams(vmem_limit_bytes=4 * 2**20),
        cost_estimate=pl.CostEstimate(flops=10**6, bytes_accessed=5 * 10**5, transcendentals=0),
        name="sum_of_arrived",
    )(arrived, after)


def local(acts, weight, moment, second, cotangent):
    crops, _, nx, ny, nz, channels = acts.shape
    field = acts.reshape(crops, nx, ny * nz, channels)
    grad_out = cotangent.reshape(field.shape)
    core = lax.axis_index("sample") % 2
    even = coords()[0] % 2 == 0
    groups = lax.axis_size("space") // (GY * GZ)
    which = jnp.full((1,), core, jnp.int32)
    member = jnp.full((1,), lax.axis_index("sample"), jnp.int32)
    inner, outer, copies = start(jnp.full((1,), even, jnp.int32), member, field, grad_out, weight)
    mine = lax.all_to_all(copies, "space", split_axis=0, concat_axis=0, tiled=True)
    below, above = swapped(inner, outer, even, GY * GZ, groups)

    faces = edges(field)

    def along(layers, own):
        pairs = zip(layers(below[:, :2]), own, layers(above[:, :2]))
        return [jnp.concatenate(three, 1) for three in pairs]

    zlo, zhi = z_halo(*along(z_layers, faces[2:]))
    ylo, yhi = y_halo(
        *(
            jnp.concatenate([face, zlo[:, :, at : at + 1], zhi[:, :, at : at + 1]], 2)
            for at, face in zip((0, 7), along(y_layers, faces[:2]))
        )
    )
    total = crops * lax.axis_size("sample") * lax.axis_size("space") * nx * ny * nz
    beside = chip_swap(mine)
    quarters = (mine, beside, core_swap(mine), core_swap(beside))
    dy = jnp.concatenate([below[:, 2:], grad_out, above[:, 2:]], 1)
    other = core_swap(mine)
    output, dz, windows, kernel = forward(
        member, field, zlo, zhi, ylo, yhi, dy, below, above, quarters
    )
    stays, leaves = weight_grad_halves(which, windows, dz, float(total) ** (-0.5))
    chip = chip_sum(stays, core_swap(leaves))
    ylo, yhi = y_halo(*y_layers(dz), chip)
    zlo, zhi = z_halo(
        *(
            jnp.concatenate([ylo[:, :, at : at + 1], face, yhi[:, :, at : at + 1]], 2)
            for at, face in zip((0, 7), z_layers(dz))
        )
    )
    arrived = lax.all_to_all(chip, "space", split_axis=0, concat_axis=0, tiled=True)
    input_grad, token = backward(dz, ylo, yhi, zlo, zhi, kernel)
    owned = sum_of_arrived(arrived, token)
    owned, across, aslant = (
        [owned + chip_swap(owned), core_swap(owned), diagonal_swap(owned)]
    )
    weight_grad = halves_joined(owned, across + aslant, core, 0)
    new_moment = 0.9 * moment + 0.1 * weight_grad
    new_second = 0.999 * second + 0.001 * weight_grad * weight_grad
    first_fix = 1.0 - 0.9**10
    second_fix = 1.0 - 0.999**10
    new_weight = weight - 0.001 * (new_moment / first_fix) / (
        jnp.sqrt(new_second / second_fix) + 1e-08
    )
    return (
        output.reshape(acts.shape),
        input_grad.reshape(acts.shape),
        weight_grad,
        new_weight,
        new_moment,
        new_second,
    )


def solution(mesh):
    in_specs = (
        P("sample", "space", None, None, None, None),
        P("space", None),
        P("space", None),
        P("space", None),
        P("sample", "space", None, None, None, None),
    )
    out_specs = (
        P("sample", "space", None, None, None, None),
        P("sample", "space", None, None, None, None),
        P("space", None),
        P("space", None),
        P("space", None),
        P("space", None),
    )
    return jax.shard_map(local, mesh=mesh, in_specs=in_specs, out_specs=out_specs, check_vma=False)
```
